128 devices in a mesh: dp: 8 (over y, core), expert: 16 (over z, x).
Axes of the slice: x: 4, y: 4, z: 4, core: 2. Of those that a mesh axis runs over, the one named last changes fastest.
Arguments:
- text: bfloat16 [16384, 5120], P(('dp', 'expert')), may hold values from -6 to 6
- patches: bfloat16 [8, 24, 24, 1408], P('dp', None, None, 'expert'), may hold values from -6 to 6
- vis_start: int32 [8], P('dp'), may hold values from 0 to 1904
- fc1: bfloat16 [4, 1408, 4096], P(None, 'expert', 'dp'), may hold values from -0.078125 to 0.078125
- fc2: bfloat16 [4096, 4096], P('expert', 'dp'), may hold values from -0.09375 to 0.09375
- proj: bfloat16 [4096, 5120], P('expert', 'dp'), may hold values from -0.09375 to 0.09375
- norm_gain: bfloat16 [5120], replicated, may hold values from 0.099609375 to 1.8984375
- router: bfloat16 [5120, 16], replicated, may hold values from -0.078125 to 0.078125
- routes: int32 [16384, 1], P(('dp', 'expert')), may hold values from 0 to 15; in each aligned block of 128 rows (0 to 127, 128 to 255, ...) at most 10 rows name the same one
- gate_w: bfloat16 [16, 5120, 4096], P('expert', None, 'dp'), may hold values from -0.15625 to 0.15625
- up_w: bfloat16 [16, 5120, 4096], P('expert', None, 'dp'), may hold values from -0.15625 to 0.15625
- down_w: bfloat16 [16, 4096, 5120], P('expert', 'dp'), may hold values from -0.09375 to 0.09375
Outputs:
- layer_out: bfloat16 [16384, 5120], P(('dp', 'expert'))
The draws below stay inside these ranges and needn't reach their ends.
Inputs may be any that keep to these rules, and one draw needn't show every extreme that they name: `routes`: among the 128 positions of one device each expert is named at most 10 times. The image of sequence n fills the 144 positions from vis_start[n] on.
All inputs are finite; a program needn't handle non-finite values.
Results may differ from the reference program's by a relative error of at most 0.024.
Values may be sent and summed in bfloat16 or wider, within the bound.
No kernel may reach another device: no remote copies, remote signals or barrier semaphores. Data moves between devices by JAX's collectives and lax.ppermute only.
A program may use at most 128 MiB of HBM per device.

```python
import math
import jax
import jax.numpy as jnp
import numpy as np
from jax import lax

D = 5120
FF = 4096
VC = 1408
VA = 4096
GRID = 24
TOK_DEV = 128
VT = 144
EXPERTS = 16
CAP = 10
SEQ = 2048
IMAGES = 8
TOKENS = 16384
N_DP = 8
DEVICES = 128


def plant(result, stream_key, low, largest):
    longest = result.shape.index(max(result.shape))
    spots = []
    for shift in (0, 1):
        where = [jax.random.randint(jax.random.fold_in(stream_key, axis), (), 0, length) for axis, length in enumerate(result.shape)]
        where[longest] = (where[longest] + shift) % result.shape[longest]
        spots.append(tuple(where))
    return result.at[spots[0]].set(low).at[spots[1]].set(largest)


def shard_levels(stream_key, extent, split, smallest, top_value):
    gain = 1.0
    for position, parts in split:
        heights = jax.random.uniform(jax.random.fold_in(jax.random.fold_in(stream_key, 6), position), (parts,), jnp.float32, smallest / len(split), top_value / len(split))
        gain = gain * jnp.repeat(jnp.exp(heights), extent[position] // parts).reshape((-1,) + (1,) * (len(extent) - 1 - position))
    return gain


def deal_out(key, own, number, rows, amount, top, bound, slope):
    ranking = jax.random.permutation(key, amount)
    heavy_load, common = load_shares(amount, rows * top, bound, slope, True), load_shares(amount, rows * top, bound, slope, False)
    places = jnp.arange(amount)

    def named(tallies, rotation):
        used = int((tallies > 0).sum())
        fixed = max(1, used // 4)
        passed = fixed + (places - fixed + rotation * (used - fixed)) % max(1, amount - fixed)
        return jnp.zeros((amount,), jnp.int32).at[ranking[jnp.where(places < fixed, places, passed)]].set(jnp.asarray(tallies, jnp.int32))

    tallies = jnp.where(number % 4 == 0, named(heavy_load, number // 4), named(common, number - number // 4 - 1))
    mixed = jax.random.permutation(jax.random.fold_in(own, 3), amount)
    source_of, taker = mixed[0:amount // 2 * 2:2], mixed[1:amount // 2 * 2:2]
    slack = jnp.minimum(tallies[source_of] - 1, bound - tallies[taker]) // 2
    slack = jnp.where((source_of == ranking[0]) | (taker == ranking[0]) | (tallies[taker] == 0), 0, jnp.maximum(slack, 0))
    passed = jax.random.randint(jax.random.fold_in(own, 4), (amount // 2,), 0, 1 << 20) % (slack + 1)
    tallies = tallies.at[source_of].add(-passed).at[taker].add(passed)
    items = jnp.searchsorted(jnp.cumsum(tallies), jnp.arange(rows * top), side="right").astype(jnp.int32)
    listing = items.reshape(top, rows).T
    listing = listing[jax.random.permutation(jax.random.fold_in(own, 1), rows)]
    rotation = jax.random.randint(jax.random.fold_in(own, 2), (rows, 1), 0, top)
    return jnp.take_along_axis(listing, (jnp.arange(top)[None, :] + rotation) % top, axis=1)


def load_shares(count, total, bound, lean, full):
    portions = [(1 << 20) // math.isqrt(rank ** lean) + 1 for rank in range(1, count + 1)]
    largest = bound if full else min(bound, max(-(-total // count), total * portions[0] // sum(portions)))
    least = 1 if total - largest >= count - 1 else 0
    counts, rest = [largest] + [least] * (count - 1), total - largest - least * (count - 1)
    while rest > 0:
        candidates = [i for i in range(1, count) if counts[i] < largest] or [i for i in range(1, count) if counts[i] < bound]
        whole, left = sum([portions[i] for i in candidates]), rest
        for i in candidates:
            extra = min(bound - counts[i], max(1, left * portions[i] // whole), rest)
            counts[i] = counts[i] + extra
            rest = rest - extra
    return np.array(counts)


def bell_draw(rng, shape, spread, reach, split=(), held_as=jnp.bfloat16):
    array = jax.random.normal(rng, shape, jnp.float32) * spread
    if len(split) > 0:
        array = shard_levels(rng, shape, split, -0.22, 0.18) * array
    return jnp.clip(array, min=-reach, max=reach).astype(held_as)


def setup_inputs(seed: int = 0) -> dict:
    splits = jax.random.split(jax.random.key(seed), 13)
    text = bell_draw(splits[0], (TOKENS, D), 1.0, 6.0, ((0, 128),))
    patches = bell_draw(splits[1], (IMAGES, GRID, GRID, VC), 1.0, 6.0, ((0, 8), (3, 16)))
    vis_start = plant(jax.random.randint(splits[2], (IMAGES,), 0, SEQ - VT + 1), jax.random.fold_in(splits[2], 1), 0, SEQ - VT).astype(jnp.int32)
    fc1 = bell_draw(splits[3], (4, VC, VA), (4 * VC) ** -0.5, 0.078125, ((1, 16), (2, 8)))
    fc2 = bell_draw(splits[4], (VA, VA), VA ** -0.5, 0.09375, ((0, 16), (1, 8)))
    proj = bell_draw(splits[5], (VA, D), VA ** -0.5, 0.09375, ((0, 16), (1, 8)))
    norm_gain = jnp.clip(1.0 + 0.18 * jax.random.normal(splits[6], (D,), jnp.float32), 0.099609375, 1.8984375).astype(jnp.bfloat16)
    router = bell_draw(splits[7], (D, EXPERTS), D ** -0.5, 0.078125)
    routes_keys = jax.random.split(jax.random.fold_in(splits[8], 1), TOKENS // TOK_DEV)
    routes_turns = jax.random.permutation(jax.random.fold_in(splits[8], 3), TOKENS // TOK_DEV)
    routes = jax.vmap(lambda own, number: deal_out(jax.random.fold_in(splits[8], 2), own, number, TOK_DEV, EXPERTS, 1, CAP, 1))(routes_keys, routes_turns).reshape((TOKENS, 1))
    gate_w = bell_draw(splits[9], (EXPERTS, D, FF), (D // 4) ** -0.5, 0.15625, ((0, 16), (2, 8)))
    up_w = bell_draw(splits[10], (EXPERTS, D, FF), (D // 4) ** -0.5, 0.15625, ((0, 16), (2, 8)))
    down_w = bell_draw(splits[11], (EXPERTS, FF, D), FF ** -0.5, 0.09375, ((0, 16), (1, 8)))
    return {"text": text, "patches": patches, "vis_start": vis_start, "fc1": fc1, "fc2": fc2, "proj": proj, "norm_gain": norm_gain, "router": router, "routes": routes, "gate_w": gate_w, "up_w": up_w, "down_w": down_w}


EPSILON = 1e-05

def expert_run(operands):
    token_rows, gate_mat, up_mat, down_mat = operands
    gate_act = jnp.dot(token_rows, gate_mat, preferred_element_type=jnp.float32)
    up_act = jnp.dot(token_rows, up_mat, preferred_element_type=jnp.float32)
    hidden = (jax.nn.silu(gate_act) * up_act).astype(jnp.bfloat16)
    slice_width = FF // N_DP
    partials = jnp.einsum('snf,nfd->nsd', hidden.reshape(-1, N_DP, slice_width).astype(jnp.float32), down_mat.reshape(N_DP, slice_width, D).astype(jnp.float32))
    rounded = lax.optimization_barrier(partials.astype(jnp.bfloat16))
    return rounded.astype(jnp.float32).sum(axis=0).astype(jnp.bfloat16)

def pick_rows(visual_rows, index_rows):
    return jnp.take(visual_rows, index_rows, axis=0)

def reference(text, patches, vis_start, fc1, fc2, proj, norm_gain, router, routes, gate_w, up_w, down_w):
    half_grid = GRID // 2
    shuffled = patches.reshape(IMAGES, half_grid, 2, half_grid, 2, VC)
    shuffled = shuffled.transpose(0, 1, 3, 2, 4, 5).reshape(IMAGES * VT, 4 * VC)
    pre_act = jnp.dot(shuffled, fc1.reshape(4 * VC, VA), preferred_element_type=jnp.float32)
    activated = jax.nn.gelu(pre_act, approximate=False).astype(jnp.bfloat16)
    middle_pre = jnp.dot(activated, fc2, preferred_element_type=jnp.float32)
    middle = jax.nn.gelu(middle_pre, approximate=False).astype(jnp.bfloat16)
    visual = jnp.dot(middle, proj, preferred_element_type=jnp.float32).astype(jnp.bfloat16)
    visual = visual.reshape(IMAGES, VT, D)
    sequences = text.reshape(IMAGES, SEQ, D)
    positions = jnp.arange(SEQ, dtype=jnp.int32)
    offsets = positions[None, :] - vis_start[:, None]
    in_image = (offsets >= 0) & (offsets < VT)
    picked = jax.vmap(pick_rows)(visual, jnp.clip(offsets, 0, VT - 1).astype(jnp.int32))
    embedded = jnp.where(in_image[:, :, None], picked, sequences).reshape(TOKENS, D)
    embed_f32 = embedded.astype(jnp.float32)
    mean_square = lax.optimization_barrier(jnp.mean(embed_f32 * embed_f32, axis=-1, keepdims=True))
    normed = (embed_f32 * lax.rsqrt(mean_square + EPSILON) * norm_gain.astype(jnp.float32)).astype(jnp.bfloat16)
    logits = jnp.dot(normed, router, preferred_element_type=jnp.float32)
    expert_id = routes[:, 0]
    one_hot = expert_id[:, None] == jnp.arange(EXPERTS, dtype=jnp.int32)[None, :]
    gate_score = jax.nn.sigmoid(lax.optimization_barrier(jnp.sum(jnp.where(one_hot, logits, 0.0), axis=-1)))
    routed_in = (normed.astype(jnp.float32) * gate_score[:, None]).astype(jnp.bfloat16)
    blocks = one_hot.astype(jnp.int32).reshape(DEVICES, TOK_DEV, EXPERTS)
    earlier = (jnp.cumsum(blocks, axis=1) - blocks).reshape(TOKENS, EXPERTS)
    slot_rank = lax.optimization_barrier(jnp.sum(jnp.where(one_hot, earlier, 0), axis=-1)).astype(jnp.int32)
    slot = jnp.arange(TOKENS, dtype=jnp.int32) // TOK_DEV * CAP + slot_rank
    buffer = jnp.zeros((EXPERTS, DEVICES * CAP, D), jnp.bfloat16).at[expert_id, slot].set(routed_in)
    outputs = lax.map(expert_run, (buffer, gate_w, up_w, down_w))
    expert_out = outputs[expert_id, slot]
    return (embed_f32 + expert_out.astype(jnp.float32)).astype(jnp.bfloat16)
```

```python
import jax
import jax.numpy as jnp
from jax import lax
from jax.sharding import PartitionSpec as P

EPSILON = 1e-05
F32 = jnp.float32
BF16 = jnp.bfloat16
I32 = jnp.int32


def mm(a, b):
    return jnp.dot(a, b, preferred_element_type=F32)


def exchange(blocks):
    return lax.all_to_all(blocks, "expert", 0, 0, tiled=True)


def cut_columns(value, size):
    rows, cols = value.shape
    return value.reshape(rows, size, cols // size).transpose(1, 0, 2)


def earlier(mask):
    n = mask.shape[-1]
    tri = (jnp.arange(n)[:, None] < jnp.arange(n)[None, :]).astype(BF16)
    return mm(mask.astype(BF16), tri).astype(I32)


def norm_and_gate(rows, norm_gain, router, expert_id):
    wide = rows.astype(F32)
    mean_square = jnp.mean(wide * wide, axis=-1, keepdims=True)
    normed = (wide * lax.rsqrt(mean_square + EPSILON) * norm_gain.astype(F32)).astype(BF16)
    logits = mm(normed, router)
    named = expert_id[:, None] == jnp.arange(router.shape[1], dtype=I32)[None, :]
    score = jax.nn.sigmoid(jnp.sum(jnp.where(named, logits, 0.0), axis=-1))
    return (normed.astype(F32) * score[:, None]).astype(BF16)


def adapter_first(patches, fc1, size):
    half = patches.shape[1] // 2
    channels = patches.shape[3]
    vis_count = half * half
    shuffled = patches.reshape(half, 2, half, 2, channels)
    shuffled = shuffled.transpose(0, 2, 1, 3, 4).reshape(vis_count, 4 * channels)
    first = lax.all_gather(fc1, "dp", axis=2, tiled=True)
    first = first.reshape(4 * channels, first.shape[2])
    return cut_columns(mm(shuffled, first).astype(BF16), size)


def activation(blocks):
    return jax.nn.gelu(jnp.sum(blocks.astype(F32), axis=0), approximate=False).astype(BF16)


def adapter_second(blocks, fc2, proj, size):
    activated = activation(blocks)
    both = lax.all_gather(jnp.concatenate([fc2, proj], axis=1), "dp", axis=0, tiled=False)
    width = fc2.shape[1]
    turn = (((1,), (1,)), ((), ()))
    part = lax.dot_general(activated, both[:, :, :width], turn, preferred_element_type=F32).astype(BF16)
    return cut_columns(part.reshape(activated.shape[0], -1), size), both[:, :, width:]


def adapter_third(blocks, third, size):
    middle = activation(blocks)
    turn = (((1,), (1,)), ((), ()))
    part = lax.dot_general(middle, third, turn, preferred_element_type=F32).astype(BF16)
    part = part.reshape(middle.shape[0], -1)
    vis_count, feature = part.shape
    row_cut, col_cut = 2, size // 2
    rows, cols = vis_count // row_cut, feature // col_cut
    blocks = part.reshape(row_cut, rows, col_cut, cols).transpose(0, 2, 1, 3)
    return blocks.reshape(size, rows, cols)


def spread_visual(mine, size):
    row_cut, col_cut = 2, size // 2
    rows, cols = mine.shape
    spread = exchange(jnp.broadcast_to(mine[None], (size, rows, cols)))
    spread = spread.reshape(row_cut, col_cut, rows, cols).transpose(0, 2, 1, 3)
    return spread.reshape(row_cut * rows, col_cut * cols)


def expert_part(rows, gate_w, up_w, down_w):
    gate_act = mm(rows, gate_w)
    up_act = mm(rows, up_w)
    hidden = (jax.nn.silu(gate_act) * up_act).astype(BF16)
    return mm(hidden, down_w).astype(BF16)


def experts(gathered, gate_w, up_w, down_w):
    partial_value = expert_part(gathered, gate_w, up_w, down_w)
    return lax.psum_scatter(partial_value, "dp", scatter_dimension=0, tiled=True)


def ring(value, step):
    size = lax.axis_size("dp")
    return lax.ppermute(value, "dp", [(i, (i + 2 * step) % size) for i in range(size)])


def swap(value):
    size = lax.axis_size("dp")
    return lax.ppermute(value, "dp", [(i, i ^ 1) for i in range(size)])


def add(*terms):
    total = terms[0].astype(F32)
    for term in terms[1:]:
        total = total + term.astype(F32)
    return total.astype(BF16)


def ring_experts(own, run):
    count = own.shape[0]
    half = count // 2
    below = ring(own, 1)
    above = ring(own, -1)
    part_own = run(jnp.concatenate([own, swap(own)]))
    far = jnp.concatenate([ring(below[:half], 1), ring(above[half:], -1)])
    near = jnp.concatenate([below, above])
    part_near = run(jnp.concatenate([near, swap(near)]))
    part_far = run(jnp.concatenate([far, swap(far)]))
    sum_own = add(part_own[:count], swap(part_own[count:]))
    sum_near = add(part_near[: 2 * count], swap(part_near[2 * count :]))
    to_below, to_above = sum_near[:count], sum_near[count:]
    from_below_low = ring(to_above[half:], 1)
    from_above_top = ring(to_below[:half], -1)
    sum_far = add(part_far[:count], swap(part_far[count:]))
    pass_up = ring(sum_far[:half], 1)
    pass_down = ring(sum_far[half:], -1)
    from_below_top = ring(add(to_above[:half], pass_up), 1)
    from_above_low = ring(add(to_below[half:], pass_down), -1)
    top = add(sum_own[:half], from_below_top, from_above_top)
    low = add(sum_own[half:], from_below_low, from_above_low)
    return jnp.concatenate([top, low])


def on_device(
    text, patches, vis_start, fc1, fc2, proj, norm_gain, router, routes, gate_w, up_w, down_w
):
    size = lax.axis_size("expert")
    me = lax.axis_index("expert")
    row_count, feature = text.shape
    experts_all = router.shape[1]
    vis_count = (patches.shape[1] // 2) ** 2
    capacity = max(2, row_count * 5 // (4 * size))
    low = capacity // 8 * 8
    high = capacity - low
    first = vis_start[0]
    expert_id = routes[:, 0]
    total = size * capacity
    rows_a = size * low
    rows_b = total - rows_a

    lanes = jnp.arange(row_count, dtype=I32)
    offsets = me * row_count + lanes - first
    in_image = (offsets >= 0) & (offsets < vis_count)
    named = jnp.arange(experts_all, dtype=I32)[:, None] == expert_id[None, :]
    named_text = named & ~in_image[None, :]
    named_img = named & in_image[None, :]
    text_total = jnp.sum(named_text.astype(I32), axis=1, keepdims=True)
    before = jnp.where(in_image[None, :], earlier(named_img) + text_total, earlier(named_text))
    rank = jnp.sum(jnp.where(named, before, 0), axis=0)
    key = jnp.where(rank < low, expert_id * low + rank, rows_a + expert_id * high + rank - low)
    slots = jnp.arange(total, dtype=I32)
    home = slots[:, None] == key[None, :]
    table = (home & ~in_image[None, :]).astype(BF16)

    routed = norm_and_gate(text, norm_gain, router, expert_id)
    out_low = mm(table[:rows_a], routed).astype(BF16).reshape(size, low, feature)
    out_high = mm(table[rows_a:], routed).astype(BF16).reshape(size, high, feature)
    spare = jnp.broadcast_to(expert_id.astype(BF16), (size, high, row_count))
    in_high = exchange(jnp.concatenate([out_high, spare], axis=2))
    in_high, out_low = lax.optimization_barrier((in_high, out_low))
    all_routes = in_high[:, 0, feature:].astype(I32).reshape(size * row_count)
    in_high = in_high[:, :, :feature].reshape(rows_b, feature)
    in_low = exchange(out_low)
    pre_blocks, in_low = lax.optimization_barrier((adapter_first(patches, fc1, size), in_low))
    in_low = in_low.reshape(rows_a, feature)
    second_blocks, third = adapter_second(exchange(pre_blocks), fc2, proj, size)

    mine = (all_routes == me).reshape(size, row_count)
    spots = jnp.arange(size * row_count, dtype=I32).reshape(size, row_count) - first
    row_image = (spots >= 0) & (spots < vis_count)
    text_count = jnp.sum((mine & ~row_image).astype(I32), axis=1)
    img_count = jnp.sum((mine & row_image).astype(I32), axis=1)
    blocks_before = jnp.arange(size)[:, None] > jnp.arange(size)[None, :]
    text_before = jnp.sum(jnp.where(blocks_before, text_count[None, :], 0), axis=1)
    img_before = jnp.sum(jnp.where(blocks_before, img_count[None, :], 0), axis=1)
    base = rows_a + jnp.maximum(jnp.sum(text_count) - rows_a, 0)
    ranks = jnp.arange(capacity, dtype=I32)[None, :]
    text_slot = ranks < text_count[:, None]
    img_slot = ~text_slot & (ranks < (text_count + img_count)[:, None])
    text_row = text_before[:, None] + ranks
    img_row = base + (img_before - text_count)[:, None] + ranks
    row_of = jnp.where(text_slot, text_row, jnp.where(img_slot, img_row, -1))
    split = lambda value: jnp.concatenate([value[:, :low].reshape(-1), value[:, low:].reshape(-1)])
    row_of_text = split(jnp.where(text_slot, text_row, -1))
    row_of = split(row_of)
    pack = (slots[:, None] == row_of_text[None, :]).astype(BF16)
    unpack = (row_of[:, None] == slots[None, :]).astype(BF16)

    chunk_a = (mm(pack[:rows_a, :rows_a], in_low) + mm(pack[:rows_a, rows_a:], in_high)).astype(BF16)
    run = lambda rows: expert_part(rows, gate_w[0], up_w[0], down_w[0])
    done_a = ring_experts(chunk_a, run)

    visual_blocks = exchange(adapter_third(exchange(second_blocks), third, size))
    visual_mine = jnp.sum(visual_blocks.astype(F32), axis=0).astype(BF16)
    visual = spread_visual(visual_mine, size)
    img_routes = lax.dynamic_slice(all_routes, (first,), (vis_count,))
    routed_img = norm_and_gate(visual, norm_gain, router, img_routes)
    mine_img = img_routes == me
    img_rank = earlier(mine_img[None, :])[0] + (base - rows_a)
    take = (jnp.arange(rows_b, dtype=I32)[:, None] == jnp.where(mine_img, img_rank, -1)[None, :]).astype(BF16)
    chunk_b = (
        mm(pack[rows_a:, :rows_a], in_low) + mm(pack[rows_a:, rows_a:], in_high) + mm(take, routed_img)
    ).astype(BF16)
    gathered_b = lax.all_gather(chunk_b, "dp", axis=0, tiled=True)
    done_b = experts(gathered_b, gate_w[0], up_w[0], down_w[0])

    back = mm(unpack[:, :rows_a], done_a) + mm(unpack[:, rows_a:], done_b)
    back = back.astype(BF16)
    back_low = exchange(back[:rows_a].reshape(size, low, feature)).reshape(rows_a, feature)
    back_high = exchange(back[rows_a:].reshape(size, high, feature)).reshape(rows_b, feature)
    turn = (((0,), (0,)), ((), ()))
    home = home.astype(BF16)
    combined = lax.dot_general(home[:rows_a], back_low, turn, preferred_element_type=F32)
    combined = combined + lax.dot_general(home[rows_a:], back_high, turn, preferred_element_type=F32)
    pick = (offsets[:, None] == jnp.arange(vis_count, dtype=I32)[None, :]).astype(BF16)
    embedded = jnp.where(in_image[:, None], mm(pick, visual), text.astype(F32))
    return (embedded + combined).astype(BF16)


def solution(mesh):
    return jax.shard_map(
        on_device,
        mesh=mesh,
        in_specs=(
            P(("dp", "expert"), None),
            P("dp", None, None, "expert"),
            P("dp"),
            P(None, "expert", "dp"),
            P("expert", "dp"),
            P("expert", "dp"),
            P(),
            P(),
            P(("dp", "expert"), None),
            P("expert", None, "dp"),
            P("expert", None, "dp"),
            P("expert", "dp", None),
        ),
        out_specs=P(("dp", "expert"), None),
        check_vma=False,
    )
```

```python
import functools

import jax
import jax.numpy as jnp
from jax import lax
from jax.experimental import pallas as pl
from jax.experimental.pallas import tpu as pltpu
from jax.sharding import PartitionSpec as P

EPSILON = 1e-05
F32 = jnp.float32
BF16 = jnp.bfloat16
I32 = jnp.int32


def mm(a, b):
    return jnp.dot(a, b, preferred_element_type=F32)


def exchange(blocks):
    return lax.all_to_all(blocks, "expert", 0, 0, tiled=True)


def cut_columns(value, size):
    rows, cols = value.shape
    return value.reshape(rows, size, cols // size).transpose(1, 0, 2)


def earlier(mask):
    n = mask.shape[-1]
    tri = (jnp.arange(n)[:, None] < jnp.arange(n)[None, :]).astype(BF16)
    return mm(mask.astype(BF16), tri).astype(I32)


def norm_and_gate(rows, norm_gain, router, expert_id):
    wide = rows.astype(F32)
    mean_square = jnp.mean(wide * wide, axis=-1, keepdims=True)
    normed = (wide * lax.rsqrt(mean_square + EPSILON) * norm_gain.astype(F32)).astype(BF16)
    logits = mm(normed, router)
    named = expert_id[:, None] == jnp.arange(router.shape[1], dtype=I32)[None, :]
    score = jax.nn.sigmoid(jnp.sum(jnp.where(named, logits, 0.0), axis=-1))
    return (normed.astype(F32) * score[:, None]).astype(BF16)


def adapter_first(patches, fc1, size):
    half = patches.shape[1] // 2
    channels = patches.shape[3]
    vis_count = half * half
    shuffled = patches.reshape(half, 2, half, 2, channels)
    shuffled = shuffled.transpose(0, 2, 1, 3, 4).reshape(vis_count, 4 * channels)
    first = lax.all_gather(fc1, "dp", axis=2, tiled=True)
    first = first.reshape(4 * channels, first.shape[2])
    return cut_columns(mm(shuffled, first).astype(BF16), size)


def layer_kernel(at, row_cut, blocks_ref, weights_ref, out_ref, active):
    @pl.when(pl.program_id(0) == 0)
    def _():
        total = blocks_ref[0].astype(F32)
        for i in range(1, blocks_ref.shape[0]):
            total += blocks_ref[i].astype(F32)
        active[...] = (0.5 * total * (1.0 + lax.erf(total * (0.5**0.5)))).astype(BF16)

    width = out_ref.shape[-1]
    if row_cut:
        rows = out_ref.shape[2]
        part = mm(active[...], weights_ref[:, at : at + width]).astype(BF16)
        for i in range(row_cut):
            out_ref[i, 0] = part[i * rows : (i + 1) * rows]
    else:
        for i in range(out_ref.shape[0]):
            out_ref[i] = mm(active[...], weights_ref[:, at + i * width : at + (i + 1) * width]).astype(BF16)


def layer(blocks, weights, at, width, row_cut):
    size, tokens, inner = blocks.shape
    parts = weights.shape[0] // inner
    if row_cut:
        shape = (row_cut, parts, tokens // row_cut, width)
        out_spec = pl.BlockSpec((row_cut, 1, tokens // row_cut, width), lambda d: (0, d, 0, 0))
    else:
        shape = (size, tokens, parts * width // size)
        out_spec = pl.BlockSpec((size // parts, tokens, parts * width // size), lambda d: (d, 0, 0))
    return pl.pallas_call(
        functools.partial(layer_kernel, at, row_cut),
        grid=(parts,),
        in_specs=[
            pl.BlockSpec(blocks.shape, lambda d: (0, 0, 0)),
            pl.BlockSpec((inner, weights.shape[1]), lambda d: (d, 0)),
        ],
        out_specs=out_spec,
        out_shape=jax.ShapeDtypeStruct(shape, BF16),
        scratch_shapes=[pltpu.VMEM((tokens, inner), BF16)],
        compiler_params=pltpu.CompilerParams(dimension_semantics=("arbitrary",), vmem_limit_bytes=16 << 20),
        cost_estimate=pl.CostEstimate(
            flops=2 * tokens * inner * parts * width,
            bytes_accessed=2 * weights.size + 4 * blocks.size,
            transcendentals=tokens * inner,
        ),
        name="layer",
    )(blocks, weights)


def token_order(blocks):
    size, rows, cols = blocks.shape
    blocks = blocks.reshape(2, size // 2, rows, cols).transpose(0, 2, 1, 3)
    return blocks.reshape(2 * rows, size // 2 * cols)


CHUNK = 1280
ROW_TILE = 256


def span(index, length):
    return pl.ds(pl.multiple_of(index * length, length), length)


def expert_kernel(in_count, *refs):
    blocks = refs[:in_count]
    weights = refs[in_count : in_count + 3]
    outs = refs[in_count + 3 : -10]
    rows, gate_v, up_v, down_v, gate_acc, up_acc, hidden, in_sem, w_sem, out_sem = refs[-10:]
    feature = rows.shape[1]
    chunks = feature // CHUNK
    tiles = rows.shape[0] // ROW_TILE

    def blocks_in():
        at = 0
        for i, block in enumerate(blocks):
            yield pltpu.make_async_copy(block, rows.at[pl.ds(at, block.shape[0])], in_sem.at[i])
            at += block.shape[0]

    def inner(which, k):
        held = (gate_v, up_v)[which]
        return pltpu.make_async_copy(weights[which].at[span(k, CHUNK)], held.at[span(k, CHUNK)], w_sem.at[which, k])

    def outer(k):
        return pltpu.make_async_copy(weights[2].at[:, span(k, CHUNK)], down_v.at[:, span(k, CHUNK)], w_sem.at[2, k])

    def leaving(k):
        at = 0
        for i, out in enumerate(outs):
            count = out.shape[0]
            yield pltpu.make_async_copy(
                rows.at[pl.ds(at, count), span(k, CHUNK)], out.at[:, span(k, CHUNK)], out_sem.at[i, k]
            )
            at += count

    for copy in blocks_in():
        copy.start()

    @pl.loop(0, chunks)
    def _(k):
        inner(0, k).start()
        inner(1, k).start()

    @pl.loop(0, chunks)
    def _(k):
        outer(k).start()

    for copy in blocks_in():
        copy.wait()
    gate_acc[...] = jnp.zeros_like(gate_acc)
    up_acc[...] = jnp.zeros_like(up_acc)

    @pl.loop(0, chunks)
    def _(k):
        inner(0, k).wait()
        inner(1, k).wait()

        @pl.loop(0, tiles)
        def _(t):
            part = rows[span(t, ROW_TILE), span(k, CHUNK)]
            gate_acc[span(t, ROW_TILE), :] += mm(part, gate_v[span(k, CHUNK), :])
            up_acc[span(t, ROW_TILE), :] += mm(part, up_v[span(k, CHUNK), :])

    hidden[...] = (jax.nn.silu(gate_acc[...]) * up_acc[...]).astype(BF16)

    @pl.loop(0, chunks)
    def _(k):
        outer(k).wait()

        @pl.loop(0, tiles)
        def _(t):
            made = mm(hidden[span(t, ROW_TILE), :], down_v[:, span(k, CHUNK)])
            rows[span(t, ROW_TILE), span(k, CHUNK)] = made.astype(BF16)

        for copy in leaving(k):
            copy.start()

    @pl.loop(0, chunks)
    def _(k):
        for copy in leaving(k):
            copy.wait()


def expert_part(blocks, out_rows, gate_w, up_w, down_w):
    feature, width = gate_w.shape
    count = sum(block.shape[0] for block in blocks)
    chunks = feature // CHUNK
    weights = [pltpu.with_memory_space_constraint(w, pltpu.HBM) for w in (gate_w, up_w, down_w)]
    anywhere = pl.BlockSpec(memory_space=pl.ANY)
    return pl.pallas_call(
        functools.partial(expert_kernel, len(blocks)),
        in_specs=[anywhere] * (len(blocks) + 3),
        out_specs=[anywhere] * len(out_rows),
        out_shape=[jax.ShapeDtypeStruct((rows, feature), BF16) for rows in out_rows],
        scratch_shapes=[
            pltpu.VMEM((count, feature), BF16),
            pltpu.VMEM((feature, width), BF16),
            pltpu.VMEM((feature, width), BF16),
            pltpu.VMEM((width, feature), BF16),
            pltpu.VMEM((count, width), F32),
            pltpu.VMEM((count, width), F32),
            pltpu.VMEM((count, width), BF16),
            pltpu.SemaphoreType.DMA((len(blocks),)),
            pltpu.SemaphoreType.DMA((3, chunks)),
            pltpu.SemaphoreType.DMA((len(out_rows), chunks)),
        ],
        compiler_params=pltpu.CompilerParams(vmem_limit_bytes=28 << 20),
        cost_estimate=pl.CostEstimate(
            flops=6 * count * feature * width,
            bytes_accessed=6 * feature * width + 4 * count * feature,
            transcendentals=count * width,
        ),
        name="expert_part",
    )(*blocks, *weights)


def ring(value, step):
    size = lax.axis_size("dp")
    return lax.ppermute(value, "dp", [(i, (i + 2 * step) % size) for i in range(size)])


def swap(value):
    size = lax.axis_size("dp")
    return lax.ppermute(value, "dp", [(i, i ^ 1) for i in range(size)])


def tie(*values):
    return lax.optimization_barrier(values)


def after(first, *values):
    return lax.optimization_barrier((*values, first))[:-1]


def add(*terms):
    total = terms[0].astype(F32)
    for term in terms[1:]:
        total = total + term.astype(F32)
    return total.astype(BF16)


def on_device(
    text, patches, vis_start, fc1, fc2, proj, norm_gain, router, routes, gate_w, up_w, down_w
):
    size = lax.axis_size("expert")
    me = lax.axis_index("expert")
    row_count, feature = text.shape
    experts_all = router.shape[1]
    vis_count = (patches.shape[1] // 2) ** 2
    capacity = max(2, row_count * 5 // (4 * size))
    first = vis_start[0]
    expert_id = routes[:, 0]
    total = size * capacity
    rows_a = size * (capacity // 8 * 8)
    rows_b = total - rows_a

    lanes = jnp.arange(row_count, dtype=I32)
    offsets = me * row_count + lanes - first
    in_image = (offsets >= 0) & (offsets < vis_count)
    named = jnp.arange(experts_all, dtype=I32)[:, None] == expert_id[None, :]
    named_text = named & ~in_image[None, :]
    named_img = named & in_image[None, :]
    text_total = jnp.sum(named_text.astype(I32), axis=1, keepdims=True)
    before = jnp.where(in_image[None, :], earlier(named_img) + text_total, earlier(named_text))
    rank = jnp.sum(jnp.where(named, before, 0), axis=0)
    key = expert_id * capacity + rank
    slots = jnp.arange(total, dtype=I32)
    home = slots[:, None] == key[None, :]

    routed = norm_and_gate(text, norm_gain, router, expert_id)
    leaving = mm((home & ~in_image[None, :]).astype(BF16), routed).astype(BF16)
    spare = jnp.broadcast_to(expert_id.astype(BF16), (size, 8, row_count))
    slab = capacity * feature // row_count
    leaving = jnp.concatenate([leaving.reshape(size, slab, row_count), spare], axis=1)
    arrived = exchange(leaving)
    all_routes = arrived[:, slab, :].astype(I32).reshape(size * row_count)
    pre_blocks, arrived = lax.optimization_barrier((adapter_first(patches, fc1, size), arrived))
    arrived = arrived[:, :slab, :].reshape(total, feature)
    later = lax.all_gather(jnp.concatenate([fc2, proj], axis=1), "dp", axis=0, tiled=True)
    second_blocks = layer(exchange(pre_blocks), later, 0, fc2.shape[1], 0)

    mine = (all_routes == me).reshape(size, row_count)
    spots = jnp.arange(size * row_count, dtype=I32).reshape(size, row_count) - first
    row_image = (spots >= 0) & (spots < vis_count)
    text_count = jnp.sum((mine & ~row_image).astype(I32), axis=1)
    img_count = jnp.sum((mine & row_image).astype(I32), axis=1)
    blocks_before = jnp.arange(size)[:, None] > jnp.arange(size)[None, :]
    text_before = jnp.sum(jnp.where(blocks_before, text_count[None, :], 0), axis=1)
    img_before = jnp.sum(jnp.where(blocks_before, img_count[None, :], 0), axis=1)
    base = rows_a + jnp.maximum(jnp.sum(text_count) - rows_a, 0)
    ranks = jnp.arange(capacity, dtype=I32)[None, :]
    text_slot = ranks < text_count[:, None]
    img_slot = ~text_slot & (ranks < (text_count + img_count)[:, None])
    text_row = text_before[:, None] + ranks
    img_row = base + (img_before - text_count)[:, None] + ranks
    row_of = jnp.where(text_slot, text_row, jnp.where(img_slot, img_row, -1))
    row_of_text = jnp.where(text_slot, text_row, -1).reshape(total)
    row_of = row_of.reshape(total)
    pack = (slots[:, None] == row_of_text[None, :]).astype(BF16)
    unpack = (row_of[:, None] == slots[None, :]).astype(BF16)

    run = lambda blocks, out_rows: expert_part(blocks, out_rows, gate_w[0], up_w[0], down_w[0])
    chunk_a = mm(pack[:rows_a], arrived).astype(BF16)
    half = rows_a // 2
    below, above, other = ring(chunk_a, 1), ring(chunk_a, -1), swap(chunk_a)
    own, other = after(second_blocks, chunk_a, other)
    mine, theirs = run([own, other], (rows_a, rows_a))
    below, above = after(theirs, below, above)
    far_top, far_low = ring(below[:half], 1), ring(above[half:], -1)
    below_pair, above_pair = swap(below), swap(above)
    second_blocks, mine, theirs = tie(exchange(second_blocks), mine, theirs)
    third_blocks = layer(second_blocks, later, fc2.shape[1], proj.shape[1], 2)
    third_blocks = third_blocks.reshape(size, vis_count // 2, proj.shape[1])

    below, above, below_pair, above_pair = after(third_blocks, below, above, below_pair, above_pair)
    below_top, below_low, below_other, above_top, above_low, above_other = run(
        [below, below_pair, above, above_pair], (half, half, rows_a, half, half, rows_a)
    )
    far_top_pair, far_low_pair = swap(far_top), swap(far_low)
    mine_too = swap(theirs)
    visual_blocks, below_other, above_other, mine_too = tie(
        exchange(third_blocks), below_other, above_other, mine_too
    )
    visual_mine = jnp.sum(visual_blocks.astype(F32), axis=0).astype(BF16)

    visual_blocks = jnp.broadcast_to(visual_mine[None], (size, *visual_mine.shape))
    far_top, far_low, far_top_pair, far_low_pair = after(
        visual_blocks, far_top, far_low, far_top_pair, far_low_pair
    )
    below_too, above_too = swap(below_other), swap(above_other)
    far_mine_top, far_mine_low, far_theirs = run(
        [far_top, far_low, far_top_pair, far_low_pair], (half, half, rows_a)
    )
    from_below_low = ring(add(above_low, above_too[half:]), 1)
    from_above_top = ring(add(below_top, below_too[:half]), -1)
    far_too = swap(far_theirs)
    visual = token_order(exchange(visual_blocks))
    visual, far_too = tie(visual, far_too)
    pass_up = ring(add(far_mine_top, far_too[:half]), 1)
    pass_down = ring(add(far_mine_low, far_too[half:]), -1)
    img_routes = lax.dynamic_slice(all_routes, (first,), (vis_count,))
    routed_img = norm_and_gate(visual, norm_gain, router, img_routes)
    mine_img = img_routes == me
    img_rank = earlier(mine_img[None, :])[0] + (base - rows_a)
    take = (jnp.arange(rows_b, dtype=I32)[:, None] == jnp.where(mine_img, img_rank, -1)[None, :]).astype(BF16)
    chunk_b = (mm(pack[rows_a:], arrived) + mm(take, routed_img)).astype(BF16)
    gathered_b = lax.all_gather(chunk_b, "dp", axis=0, tiled=True)
    gathered_b, pass_up, pass_down = tie(gathered_b, pass_up, pass_down)
    from_below_top = ring(add(above_top, above_too[:half], pass_up), 1)
    from_above_low = ring(add(below_low, below_too[half:], pass_down), -1)
    (part_b,) = run([gathered_b], (gathered_b.shape[0],))
    done_b = lax.psum_scatter(part_b, "dp", scatter_dimension=0, tiled=True)
    top = add(mine[:half], mine_too[:half], from_below_top, from_above_top)
    low = add(mine[half:], mine_too[half:], from_below_low, from_above_low)
    done_a = jnp.concatenate([top, low])

    back = (mm(unpack[:, :rows_a], done_a) + mm(unpack[:, rows_a:], done_b)).astype(BF16)
    back = exchange(back.reshape(size, slab, row_count)).reshape(total, feature)
    turn = (((0,), (0,)), ((), ()))
    combined = lax.dot_general(home.astype(BF16), back, turn, preferred_element_type=F32)
    pick = (offsets[:, None] == jnp.arange(vis_count, dtype=I32)[None, :]).astype(BF16)
    embedded = jnp.where(in_image[:, None], mm(pick, visual), text.astype(F32))
    return (embedded + combined).astype(BF16)


def solution(mesh):
    return jax.shard_map(
        on_device,
        mesh=mesh,
        in_specs=(
            P(("dp", "expert"), None),
            P("dp", None, None, "expert"),
            P("dp"),
            P(None, "expert", "dp"),
            P("expert", "dp"),
            P("expert", "dp"),
            P(),
            P(),
            P(("dp", "expert"), None),
            P("expert", None, "dp"),
            P("expert", None, "dp"),
            P("expert", "dp", None),
        ),
        out_specs=P(("dp", "expert"), None),
        check_vma=False,
    )
```

```python
import functools

import jax
import jax.numpy as jnp
from jax import lax
from jax.experimental import pallas as pl
from jax.experimental.pallas import tpu as pltpu
from jax.sharding import PartitionSpec as P

EPSILON = 1e-05
F32 = jnp.float32
BF16 = jnp.bfloat16
I32 = jnp.int32


def mm(a, b):
    return jnp.dot(a, b, preferred_element_type=F32)


def exchange(blocks):
    return lax.all_to_all(blocks, "expert", 0, 0, tiled=True)


def cut_columns(value, size):
    rows, cols = value.shape
    return value.reshape(rows, size, cols // size).transpose(1, 0, 2)


def earlier(mask):
    n = mask.shape[-1]
    tri = (jnp.arange(n)[:, None] < jnp.arange(n)[None, :]).astype(BF16)
    return mm(mask.astype(BF16), tri).astype(I32)


def norm_and_gate(rows, norm_gain, router, expert_id):
    wide = rows.astype(F32)
    mean_square = jnp.mean(wide * wide, axis=-1, keepdims=True)
    normed = (wide * lax.rsqrt(mean_square + EPSILON) * norm_gain.astype(F32)).astype(BF16)
    logits = mm(normed, router)
    named = expert_id[:, None] == jnp.arange(router.shape[1], dtype=I32)[None, :]
    score = jax.nn.sigmoid(jnp.sum(jnp.where(named, logits, 0.0), axis=-1))
    return (normed.astype(F32) * score[:, None]).astype(BF16)


def adapter_first(patches, fc1, size):
    half = patches.shape[1] // 2
    channels = patches.shape[3]
    vis_count = half * half
    shuffled = patches.reshape(half, 2, half, 2, channels)
    shuffled = shuffled.transpose(0, 2, 1, 3, 4).reshape(vis_count, 4 * channels)
    first = lax.all_gather(fc1, "dp", axis=2, tiled=True)
    first = first.reshape(4 * channels, first.shape[2])
    return cut_columns(mm(shuffled, first).astype(BF16), size)


def layer_kernel(at, blocks_ref, weights_ref, out_ref, active, held, sems):
    parts, inner, width = held.shape

    def columns(d):
        rows = pl.ds(pl.multiple_of(d * inner, inner), inner)
        return pltpu.make_async_copy(weights_ref.at[rows, pl.ds(at, width)], held.at[d], sems.at[d])

    @pl.loop(0, parts)
    def _(d):
        columns(d).start()

    total = blocks_ref[0].astype(F32)
    for i in range(1, blocks_ref.shape[0]):
        total += blocks_ref[i].astype(F32)
    active[...] = (0.5 * total * (1.0 + lax.erf(total * (0.5**0.5)))).astype(BF16)
    size, rows, cols = out_ref.shape

    @pl.loop(0, parts)
    def _(d):
        columns(d).wait()
        part = mm(active[...], held[d]).astype(BF16)
        for i in range(size // parts):
            if cols == width:
                out_ref[i * parts + d] = part[i * rows : (i + 1) * rows]
            else:
                out_ref[d * (size // parts) + i] = part[:, i * cols : (i + 1) * cols]


def layer(blocks, weights, at, width, row_cut):
    size, tokens, inner = blocks.shape
    parts = weights.shape[0] // inner
    shape = (size, tokens // row_cut, parts * width * row_cut // size)
    return pl.pallas_call(
        functools.partial(layer_kernel, at),
        in_specs=[pl.BlockSpec(memory_space=pltpu.VMEM), pl.BlockSpec(memory_space=pl.ANY)],
        out_specs=pl.BlockSpec(memory_space=pltpu.VMEM),
        out_shape=jax.ShapeDtypeStruct(shape, BF16),
        scratch_shapes=[
            pltpu.VMEM((tokens, inner), BF16),
            pltpu.VMEM((parts, inner, width), BF16),
            pltpu.SemaphoreType.DMA((parts,)),
        ],
        compiler_params=pltpu.CompilerParams(vmem_limit_bytes=16 << 20),
        cost_estimate=pl.CostEstimate(
            flops=2 * tokens * inner * parts * width,
            bytes_accessed=2 * inner * parts * width + 4 * blocks.size,
            transcendentals=tokens * inner,
        ),
        name="layer",
    )(blocks, pltpu.with_memory_space_constraint(weights, pltpu.HBM))


def visual_kernel(blocks_ref, gain_ref, router_ref, named_ref, take_ref, base_ref, visual_ref, chunk_ref):
    size, rows, cols = blocks_ref.shape
    halves = visual_ref.shape[0] // rows
    across = size // halves
    parts = [
        jnp.concatenate([blocks_ref[r * across + c].astype(F32) for c in range(across)], axis=1)
        for r in range(halves)
    ]
    wide = jnp.concatenate(parts, axis=0)
    visual_ref[...] = wide.astype(BF16)
    mean_square = jnp.mean(wide * wide, axis=-1, keepdims=True)
    normed = (wide * lax.rsqrt(mean_square + EPSILON) * gain_ref[...].astype(F32)).astype(BF16)
    logits = mm(normed, router_ref[...])
    score = jax.nn.sigmoid(jnp.sum(named_ref[...] * logits, axis=-1, keepdims=True))
    routed = (normed.astype(F32) * score).astype(BF16)
    chunk_ref[...] = (base_ref[...].astype(F32) + mm(take_ref[...], routed)).astype(BF16)


def visual_chunk(blocks, norm_gain, router, named, take, base):
    size, rows, cols = blocks.shape
    feature = router.shape[0]
    tokens = size * rows * cols // feature
    return pl.pallas_call(
        visual_kernel,
        in_specs=[pl.BlockSpec(memory_space=pltpu.VMEM)] * 6,
        out_specs=[pl.BlockSpec(memory_space=pltpu.VMEM)] * 2,
        out_shape=[
            jax.ShapeDtypeStruct((tokens, feature), BF16),
            jax.ShapeDtypeStruct((take.shape[0], feature), BF16),
        ],
        compiler_params=pltpu.CompilerParams(vmem_limit_bytes=24 << 20),
        cost_estimate=pl.CostEstimate(
            flops=2 * tokens * feature * 64, bytes_accessed=8 * tokens * feature, transcendentals=tokens
        ),
        name="visual_chunk",
    )(blocks, norm_gain[None, :], router, named, take, base)


CHUNK = 1280
ROW_TILE = 256


def span(index, length):
    return pl.ds(pl.multiple_of(index * length, length), length)


def expert_kernel(in_count, *refs):
    blocks = refs[:in_count]
    weights = refs[in_count : in_count + 3]
    outs = refs[in_count + 3 : -10]
    rows, gate_v, up_v, down_v, gate_acc, up_acc, hidden, in_sem, w_sem, out_sem = refs[-10:]
    feature = rows.shape[1]
    chunks = feature // CHUNK
    tiles = rows.shape[0] // ROW_TILE

    def blocks_in():
        at = 0
        for i, block in enumerate(blocks):
            yield pltpu.make_async_copy(block, rows.at[pl.ds(at, block.shape[0])], in_sem.at[i])
            at += block.shape[0]

    def inner(which, k):
        held = (gate_v, up_v)[which]
        return pltpu.make_async_copy(weights[which].at[span(k, CHUNK)], held.at[span(k, CHUNK)], w_sem.at[which, k])

    def outer(k):
        return pltpu.make_async_copy(weights[2].at[:, span(k, CHUNK)], down_v.at[:, span(k, CHUNK)], w_sem.at[2, k])

    def leaving(k):
        at = 0
        for i, out in enumerate(outs):
            count = out.shape[0]
            yield pltpu.make_async_copy(
                rows.at[pl.ds(at, count), span(k, CHUNK)], out.at[:, span(k, CHUNK)], out_sem.at[i, k]
            )
            at += count

    for copy in blocks_in():
        copy.start()

    @pl.loop(0, chunks)
    def _(k):
        inner(0, k).start()
        inner(1, k).start()

    @pl.loop(0, chunks)
    def _(k):
        outer(k).start()

    for copy in blocks_in():
        copy.wait()
    gate_acc[...] = jnp.zeros_like(gate_acc)
    up_acc[...] = jnp.zeros_like(up_acc)

    @pl.loop(0, chunks)
    def _(k):
        inner(0, k).wait()
        inner(1, k).wait()

        @pl.loop(0, tiles)
        def _(t):
            part = rows[span(t, ROW_TILE), span(k, CHUNK)]
            gate_acc[span(t, ROW_TILE), :] += mm(part, gate_v[span(k, CHUNK), :])
            up_acc[span(t, ROW_TILE), :] += mm(part, up_v[span(k, CHUNK), :])

    hidden[...] = (jax.nn.silu(gate_acc[...]) * up_acc[...]).astype(BF16)

    @pl.loop(0, chunks)
    def _(k):
        outer(k).wait()

        @pl.loop(0, tiles)
        def _(t):
            made = mm(hidden[span(t, ROW_TILE), :], down_v[:, span(k, CHUNK)])
            rows[span(t, ROW_TILE), span(k, CHUNK)] = made.astype(BF16)

        for copy in leaving(k):
            copy.start()

    @pl.loop(0, chunks)
    def _(k):
        for copy in leaving(k):
            copy.wait()


def expert_part(blocks, out_rows, gate_w, up_w, down_w):
    feature, width = gate_w.shape
    count = sum(block.shape[0] for block in blocks)
    chunks = feature // CHUNK
    weights = [pltpu.with_memory_space_constraint(w, pltpu.HBM) for w in (gate_w, up_w, down_w)]
    anywhere = pl.BlockSpec(memory_space=pl.ANY)
    return pl.pallas_call(
        functools.partial(expert_kernel, len(blocks)),
        in_specs=[anywhere] * (len(blocks) + 3),
        out_specs=[pl.BlockSpec(memory_space=pltpu.HBM)] * len(out_rows),
        out_shape=[pltpu.HBM((rows, feature), BF16) for rows in out_rows],
        scratch_shapes=[
            pltpu.VMEM((count, feature), BF16),
            pltpu.VMEM((feature, width), BF16),
            pltpu.VMEM((feature, width), BF16),
            pltpu.VMEM((width, feature), BF16),
            pltpu.VMEM((count, width), F32),
            pltpu.VMEM((count, width), F32),
            pltpu.VMEM((count, width), BF16),
            pltpu.SemaphoreType.DMA((len(blocks),)),
            pltpu.SemaphoreType.DMA((3, chunks)),
            pltpu.SemaphoreType.DMA((len(out_rows), chunks)),
        ],
        compiler_params=pltpu.CompilerParams(vmem_limit_bytes=28 << 20),
        cost_estimate=pl.CostEstimate(
            flops=6 * count * feature * width,
            bytes_accessed=6 * feature * width + 4 * count * feature,
            transcendentals=count * width,
        ),
        name="expert_part",
    )(*[pltpu.with_memory_space_constraint(block, pltpu.HBM) for block in blocks], *weights)


def ring(value, step):
    size = lax.axis_size("dp")
    return lax.ppermute(value, "dp", [(i, (i + 2 * step) % size) for i in range(size)])


def swap(value):
    size = lax.axis_size("dp")
    return lax.ppermute(value, "dp", [(i, i ^ 1) for i in range(size)])


def tie(*values):
    return lax.optimization_barrier(values)


def after(first, *values):
    return lax.optimization_barrier((*values, first))[:-1]


def add(*terms):
    total = terms[0].astype(F32)
    for term in terms[1:]:
        total = total + term.astype(F32)
    return total.astype(BF16)


def on_device(
    text, patches, vis_start, fc1, fc2, proj, norm_gain, router, routes, gate_w, up_w, down_w
):
    size = lax.axis_size("expert")
    me = lax.axis_index("expert")
    row_count, feature = text.shape
    experts_all = router.shape[1]
    vis_count = (patches.shape[1] // 2) ** 2
    capacity = max(2, row_count * 5 // (4 * size))
    first = vis_start[0]
    expert_id = routes[:, 0]
    total = size * capacity
    rows_a = size * (capacity // 8 * 8)
    rows_b = total - rows_a

    lanes = jnp.arange(row_count, dtype=I32)
    offsets = me * row_count + lanes - first
    in_image = (offsets >= 0) & (offsets < vis_count)
    named = jnp.arange(experts_all, dtype=I32)[:, None] == expert_id[None, :]
    named_text = named & ~in_image[None, :]
    named_img = named & in_image[None, :]
    text_total = jnp.sum(named_text.astype(I32), axis=1, keepdims=True)
    before = jnp.where(in_image[None, :], earlier(named_img) + text_total, earlier(named_text))
    rank = jnp.sum(jnp.where(named, before, 0), axis=0)
    key = expert_id * capacity + rank
    slots = jnp.arange(total, dtype=I32)
    home = slots[:, None] == key[None, :]

    routed = norm_and_gate(text, norm_gain, router, expert_id)
    leaving = mm((home & ~in_image[None, :]).astype(BF16), routed).astype(BF16)
    spare = jnp.broadcast_to(expert_id.astype(BF16), (size, 8, row_count))
    slab = capacity * feature // row_count
    leaving = jnp.concatenate([leaving.reshape(size, slab, row_count), spare], axis=1)
    arrived = exchange(leaving)
    pre_blocks, arrived = lax.optimization_barrier((adapter_first(patches, fc1, size), arrived))
    all_routes = arrived[:, slab, :].astype(I32).reshape(size * row_count)
    arrived = arrived[:, :slab, :].reshape(total, feature)
    later = lax.all_gather(
        jnp.concatenate(after(leaving, fc2, proj), axis=1), "dp", axis=0, tiled=True
    )
    second_blocks = layer(exchange(pre_blocks), later, 0, fc2.shape[1], 1)

    mine = (all_routes == me).reshape(size, row_count)
    spots = jnp.arange(size * row_count, dtype=I32).reshape(size, row_count) - first
    row_image = (spots >= 0) & (spots < vis_count)
    text_count = jnp.sum((mine & ~row_image).astype(I32), axis=1)
    img_count = jnp.sum((mine & row_image).astype(I32), axis=1)
    blocks_before = jnp.arange(size)[:, None] > jnp.arange(size)[None, :]
    text_before = jnp.sum(jnp.where(blocks_before, text_count[None, :], 0), axis=1)
    img_before = jnp.sum(jnp.where(blocks_before, img_count[None, :], 0), axis=1)
    base = rows_a + jnp.maximum(jnp.sum(text_count) - rows_a, 0)
    ranks = jnp.arange(capacity, dtype=I32)[None, :]
    text_slot = ranks < text_count[:, None]
    img_slot = ~text_slot & (ranks < (text_count + img_count)[:, None])
    text_row = text_before[:, None] + ranks
    img_row = base + (img_before - text_count)[:, None] + ranks
    row_of = jnp.where(text_slot, text_row, jnp.where(img_slot, img_row, -1))
    row_of_text = jnp.where(text_slot, text_row, -1).reshape(total)
    row_of = row_of.reshape(total)
    pack = (slots[:, None] == row_of_text[None, :]).astype(BF16)
    unpack = (row_of[:, None] == slots[None, :]).astype(BF16)

    run = lambda blocks, out_rows: expert_part(blocks, out_rows, gate_w[0], up_w[0], down_w[0])
    chunk_a = mm(pack[:rows_a], arrived).astype(BF16)
    half = rows_a // 2
    below, above, other = ring(chunk_a, 1), ring(chunk_a, -1), swap(chunk_a)
    own, other = after(second_blocks, chunk_a, other)
    mine, theirs = run([own, other], (rows_a, rows_a))
    below, above = after(theirs, below, above)
    far_top, far_low = ring(below[:half], 1), ring(above[half:], -1)
    below_pair, above_pair = swap(below), swap(above)
    second_blocks, mine, theirs = tie(exchange(second_blocks), mine, theirs)
    third_blocks = layer(second_blocks, later, fc2.shape[1], proj.shape[1], 2)

    below, above, below_pair, above_pair, far_top, far_low = after(
        third_blocks, below, above, below_pair, above_pair, far_top, far_low
    )
    below_top, below_low, below_other, above_top, above_low, above_other = run(
        [below, below_pair, above, above_pair], (half, half, rows_a, half, half, rows_a)
    )
    far_top_pair, far_low_pair = swap(far_top), swap(far_low)
    mine_too = swap(theirs)
    visual_blocks, below_other, above_other, mine_too = tie(
        exchange(third_blocks), below_other, above_other, mine_too
    )
    visual_mine = jnp.sum(visual_blocks.astype(F32), axis=0).astype(BF16)

    visual_blocks = jnp.broadcast_to(visual_mine[None], (size, *visual_mine.shape))
    below_too, above_too = after(visual_blocks, swap(below_other), swap(above_other))
    to_above, to_below = add(above_low, above_too[half:]), add(below_top, below_too[:half])
    from_below_low, from_above_top = ring(to_above, 1), ring(to_below, -1)
    far = after(visual_blocks, far_top, far_low, far_top_pair, far_low_pair)
    far_mine_top, far_mine_low, far_theirs = run(far, (half, half, rows_a))
    visual_blocks, far_theirs, from_below_low, from_above_top = tie(
        exchange(visual_blocks), far_theirs, from_below_low, from_above_top
    )
    far_too = swap(far_theirs)
    pass_up = ring(add(far_mine_top, far_too[:half]), 1)
    pass_down = ring(add(far_mine_low, far_too[half:]), -1)
    img_routes = lax.dynamic_slice(all_routes, (first,), (vis_count,))
    named_img = (img_routes[:, None] == jnp.arange(experts_all, dtype=I32)[None, :]).astype(F32)
    mine_img = img_routes == me
    img_rank = earlier(mine_img[None, :])[0] + (base - rows_a)
    take = (jnp.arange(rows_b, dtype=I32)[:, None] == jnp.where(mine_img, img_rank, -1)[None, :]).astype(BF16)
    overflow = mm(pack[rows_a:], arrived).astype(BF16)
    visual, chunk_b = visual_chunk(visual_blocks, norm_gain, router, named_img, take, overflow)
    gathered_b = lax.all_gather(chunk_b, "dp", axis=0, tiled=True)
    on_above = add(above_top, above_too[:half], pass_up)
    on_below = add(below_low, below_too[half:], pass_down)
    gathered_b, on_above, on_below = tie(gathered_b, on_above, on_below)
    from_below_top, from_above_low = ring(on_above, 1), ring(on_below, -1)
    (part_b,) = run([gathered_b], (gathered_b.shape[0],))
    done_b = lax.psum_scatter(part_b, "dp", scatter_dimension=0, tiled=True)
    top = add(mine[:half], mine_too[:half], from_below_top, from_above_top)
    low = add(mine[half:], mine_too[half:], from_below_low, from_above_low)
    done_a = jnp.concatenate([top, low])

    back = (mm(unpack[:, :rows_a], done_a) + mm(unpack[:, rows_a:], done_b)).astype(BF16)
    back = exchange(back.reshape(size, slab, row_count)).reshape(total, feature)
    turn = (((0,), (0,)), ((), ()))
    combined = lax.dot_general(home.astype(BF16), back, turn, preferred_element_type=F32)
    pick = (offsets[:, None] == jnp.arange(vis_count, dtype=I32)[None, :]).astype(BF16)
    embedded = jnp.where(in_image[:, None], mm(pick, visual), text.astype(F32))
    return (embedded + combined).astype(BF16)


def solution(mesh):
    return jax.shard_map(
        on_device,
        mesh=mesh,
        in_specs=(
            P(("dp", "expert"), None),
            P("dp", None, None, "expert"),
            P("dp"),
            P(None, "expert", "dp"),
            P("expert", "dp"),
            P("expert", "dp"),
            P(),
            P(),
            P(("dp", "expert"), None),
            P("expert", None, "dp"),
            P("expert", None, "dp"),
            P("expert", "dp", None),
        ),
        out_specs=P(("dp", "expert"), None),
        check_vma=False,
    )
```

```python
import functools

import jax
import jax.numpy as jnp
from jax import lax
from jax.experimental import pallas as pl
from jax.experimental.pallas import tpu as pltpu
from jax.sharding import PartitionSpec as P

EPSILON = 1e-05
F32 = jnp.float32
BF16 = jnp.bfloat16
I32 = jnp.int32


def mm(a, b):
    return jnp.dot(a, b, preferred_element_type=F32)


def exchange(blocks):
    return lax.all_to_all(blocks, "expert", 0, 0, tiled=True)


def cut_columns(value, size):
    rows, cols = value.shape
    return value.reshape(rows, size, cols // size).transpose(1, 0, 2)


def earlier(mask):
    n = mask.shape[-1]
    tri = (jnp.arange(n)[:, None] < jnp.arange(n)[None, :]).astype(BF16)
    return mm(mask.astype(BF16), tri).astype(I32)


def norm_and_gate(rows, norm_gain, router, expert_id):
    wide = rows.astype(F32)
    mean_square = jnp.mean(wide * wide, axis=-1, keepdims=True)
    normed = (wide * lax.rsqrt(mean_square + EPSILON) * norm_gain.astype(F32)).astype(BF16)
    logits = mm(normed, router)
    named = expert_id[:, None] == jnp.arange(router.shape[1], dtype=I32)[None, :]
    score = jax.nn.sigmoid(jnp.sum(jnp.where(named, logits, 0.0), axis=-1))
    return (normed.astype(F32) * score[:, None]).astype(BF16)


def adapter_first(patches, fc1, size):
    half = patches.shape[1] // 2
    channels = patches.shape[3]
    vis_count = half * half
    shuffled = patches.reshape(half, 2, half, 2, channels)
    shuffled = shuffled.transpose(0, 2, 1, 3, 4).reshape(vis_count, 4 * channels)
    first = lax.all_gather(fc1, "dp", axis=2, tiled=True)
    first = first.reshape(4 * channels, first.shape[2])
    return cut_columns(mm(shuffled, first).astype(BF16), size)


def layer_kernel(at, blocks_ref, weights_ref, out_ref, active, held, sems):
    parts, inner, width = held.shape

    def columns(d):
        rows = pl.ds(pl.multiple_of(d * inner, inner), inner)
        return pltpu.make_async_copy(weights_ref.at[rows, pl.ds(at, width)], held.at[d], sems.at[d])

    @pl.loop(0, parts)
    def _(d):
        columns(d).start()

    total = blocks_ref[0].astype(F32)
    for i in range(1, blocks_ref.shape[0]):
        total += blocks_ref[i].astype(F32)
    active[...] = (0.5 * total * (1.0 + lax.erf(total * (0.5**0.5)))).astype(BF16)
    size, rows, cols = out_ref.shape

    @pl.loop(0, parts)
    def _(d):
        columns(d).wait()
        part = mm(active[...], held[d]).astype(BF16)
        for i in range(size // parts):
            if cols == width:
                out_ref[i * parts + d] = part[i * rows : (i + 1) * rows]
            else:
                out_ref[d * (size // parts) + i] = part[:, i * cols : (i + 1) * cols]


def layer(blocks, weights, at, width, row_cut):
    size, tokens, inner = blocks.shape
    parts = weights.shape[0] // inner
    shape = (size, tokens // row_cut, parts * width * row_cut // size)
    return pl.pallas_call(
        functools.partial(layer_kernel, at),
        in_specs=[pl.BlockSpec(memory_space=pltpu.VMEM), pl.BlockSpec(memory_space=pl.ANY)],
        out_specs=pl.BlockSpec(memory_space=pltpu.VMEM),
        out_shape=jax.ShapeDtypeStruct(shape, BF16),
        scratch_shapes=[
            pltpu.VMEM((tokens, inner), BF16),
            pltpu.VMEM((parts, inner, width), BF16),
            pltpu.SemaphoreType.DMA((parts,)),
        ],
        compiler_params=pltpu.CompilerParams(vmem_limit_bytes=16 << 20),
        cost_estimate=pl.CostEstimate(
            flops=2 * tokens * inner * parts * width,
            bytes_accessed=2 * inner * parts * width + 4 * blocks.size,
            transcendentals=tokens * inner,
        ),
        name="layer",
    )(blocks, pltpu.with_memory_space_constraint(weights, pltpu.HBM))


def visual_kernel(blocks_ref, gain_ref, router_ref, named_ref, take_ref, base_ref, visual_ref, chunk_ref):
    size, rows, cols = blocks_ref.shape
    halves = visual_ref.shape[0] // rows
    across = size // halves
    parts = [
        jnp.concatenate([blocks_ref[r * across + c].astype(F32) for c in range(across)], axis=1)
        for r in range(halves)
    ]
    wide = jnp.concatenate(parts, axis=0)
    visual_ref[...] = wide.astype(BF16)
    mean_square = jnp.mean(wide * wide, axis=-1, keepdims=True)
    normed = (wide * lax.rsqrt(mean_square + EPSILON) * gain_ref[...].astype(F32)).astype(BF16)
    turn = (((1,), (1,)), ((), ()))
    logits = lax.dot_general(normed, router_ref[...], turn, preferred_element_type=F32)
    score = jax.nn.sigmoid(jnp.sum(named_ref[...] * logits, axis=-1, keepdims=True))
    routed = (normed.astype(F32) * score).astype(BF16)
    chunk_ref[...] = (base_ref[...].astype(F32) + mm(take_ref[...], routed)).astype(BF16)


def visual_chunk(blocks, norm_gain, router, named, take, base):
    size, rows, cols = blocks.shape
    feature = router.shape[0]
    tokens = size * rows * cols // feature
    return pl.pallas_call(
        visual_kernel,
        in_specs=[pl.BlockSpec(memory_space=pltpu.VMEM)] * 6,
        out_specs=[pl.BlockSpec(memory_space=pltpu.VMEM)] * 2,
        out_shape=[
            jax.ShapeDtypeStruct((tokens, feature), BF16),
            jax.ShapeDtypeStruct((take.shape[0], feature), BF16),
        ],
        compiler_params=pltpu.CompilerParams(vmem_limit_bytes=24 << 20),
        cost_estimate=pl.CostEstimate(
            flops=2 * tokens * feature * 64, bytes_accessed=8 * tokens * feature, transcendentals=tokens
        ),
        name="visual_chunk",
    )(blocks, norm_gain[None, :], router.T, named, take, base)


CHUNK = 1280
ROW_TILE = 256


def span(index, length):
    return pl.ds(pl.multiple_of(index * length, length), length)


def expert_kernel(in_count, *refs):
    blocks = refs[:in_count]
    weights = refs[in_count : in_count + 3]
    outs = refs[in_count + 3 : -10]
    rows, gate_v, up_v, down_v, gate_acc, up_acc, hidden, in_sem, w_sem, out_sem = refs[-10:]
    feature = rows.shape[1]
    chunks = feature // CHUNK
    tiles = rows.shape[0] // ROW_TILE

    def blocks_in():
        at = 0
        for i, block in enumerate(blocks):
            yield pltpu.make_async_copy(block, rows.at[pl.ds(at, block.shape[0])], in_sem.at[i])
            at += block.shape[0]

    def inner(which, k):
        held = (gate_v, up_v)[which]
        return pltpu.make_async_copy(weights[which].at[span(k, CHUNK)], held.at[span(k, CHUNK)], w_sem.at[which, k])

    def outer(k):
        return pltpu.make_async_copy(weights[2].at[:, span(k, CHUNK)], down_v.at[:, span(k, CHUNK)], w_sem.at[2, k])

    def leaving(k):
        at = 0
        for i, out in enumerate(outs):
            count = out.shape[0]
            yield pltpu.make_async_copy(
                rows.at[pl.ds(at, count), span(k, CHUNK)], out.at[:, span(k, CHUNK)], out_sem.at[i, k]
            )
            at += count

    for copy in blocks_in():
        copy.start()

    @pl.loop(0, chunks)
    def _(k):
        inner(0, k).start()
        inner(1, k).start()

    @pl.loop(0, chunks)
    def _(k):
        outer(k).start()

    for copy in blocks_in():
        copy.wait()
    gate_acc[...] = jnp.zeros_like(gate_acc)
    up_acc[...] = jnp.zeros_like(up_acc)

    @pl.loop(0, chunks)
    def _(k):
        inner(0, k).wait()
        inner(1, k).wait()

        @pl.loop(0, tiles)
        def _(t):
            part = rows[span(t, ROW_TILE), span(k, CHUNK)]
            gate_acc[span(t, ROW_TILE), :] += mm(part, gate_v[span(k, CHUNK), :])
            up_acc[span(t, ROW_TILE), :] += mm(part, up_v[span(k, CHUNK), :])

    hidden[...] = (jax.nn.silu(gate_acc[...]) * up_acc[...]).astype(BF16)

    @pl.loop(0, chunks)
    def _(k):
        outer(k).wait()

        @pl.loop(0, tiles)
        def _(t):
            made = mm(hidden[span(t, ROW_TILE), :], down_v[:, span(k, CHUNK)])
            rows[span(t, ROW_TILE), span(k, CHUNK)] = made.astype(BF16)

        for copy in leaving(k):
            copy.start()

    @pl.loop(0, chunks)
    def _(k):
        for copy in leaving(k):
            copy.wait()


def expert_part(blocks, out_rows, gate_w, up_w, down_w, share=1):
    feature, width = gate_w.shape
    count = sum(block.shape[0] for block in blocks)
    chunks = feature // CHUNK
    weights = [pltpu.with_memory_space_constraint(w, pltpu.HBM) for w in (gate_w, up_w, down_w)]
    anywhere = pl.BlockSpec(memory_space=pl.ANY)
    return pl.pallas_call(
        functools.partial(expert_kernel, len(blocks)),
        in_specs=[anywhere] * (len(blocks) + 3),
        out_specs=[pl.BlockSpec(memory_space=pltpu.HBM)] * len(out_rows),
        out_shape=[pltpu.HBM((rows, feature), BF16) for rows in out_rows],
        scratch_shapes=[
            pltpu.VMEM((count, feature), BF16),
            pltpu.VMEM((feature, width), BF16),
            pltpu.VMEM((feature, width), BF16),
            pltpu.VMEM((width, feature), BF16),
            pltpu.VMEM((count, width), F32),
            pltpu.VMEM((count, width), F32),
            pltpu.VMEM((count, width), BF16),
            pltpu.SemaphoreType.DMA((len(blocks),)),
            pltpu.SemaphoreType.DMA((3, chunks)),
            pltpu.SemaphoreType.DMA((len(out_rows), chunks)),
        ],
        compiler_params=pltpu.CompilerParams(vmem_limit_bytes=28 << 20),
        cost_estimate=pl.CostEstimate(
            flops=6 * count * feature * width // share,
            bytes_accessed=(6 * feature * width + 4 * count * feature) // share,
            transcendentals=count * width // share,
        ),
        name="expert_part",
    )(*[pltpu.with_memory_space_constraint(block, pltpu.HBM) for block in blocks], *weights)


def ring(value, step):
    size = lax.axis_size("dp")
    return lax.ppermute(value, "dp", [(i, (i + 2 * step) % size) for i in range(size)])


def swap(value):
    size = lax.axis_size("dp")
    return lax.ppermute(value, "dp", [(i, i ^ 1) for i in range(size)])


def tie(*values):
    return lax.optimization_barrier(values)


def after(first, *values):
    return lax.optimization_barrier((*values, first))[:-1]


def add(*terms):
    total = terms[0].astype(F32)
    for term in terms[1:]:
        total = total + term.astype(F32)
    return total.astype(BF16)


def on_device(
    text, patches, vis_start, fc1, fc2, proj, norm_gain, router, routes, gate_w, up_w, down_w
):
    size = lax.axis_size("expert")
    me = lax.axis_index("expert")
    row_count, feature = text.shape
    experts_all = router.shape[1]
    vis_count = (patches.shape[1] // 2) ** 2
    capacity = max(2, row_count * 5 // (4 * size))
    first = vis_start[0]
    expert_id = routes[:, 0]
    total = size * capacity
    rows_a = size * (capacity // 8 * 8)
    rows_b = total - rows_a

    lanes = jnp.arange(row_count, dtype=I32)
    offsets = me * row_count + lanes - first
    in_image = (offsets >= 0) & (offsets < vis_count)
    named = jnp.arange(experts_all, dtype=I32)[:, None] == expert_id[None, :]
    named_text = named & ~in_image[None, :]
    named_img = named & in_image[None, :]
    text_total = jnp.sum(named_text.astype(I32), axis=1, keepdims=True)
    before = jnp.where(in_image[None, :], earlier(named_img) + text_total, earlier(named_text))
    rank = jnp.sum(jnp.where(named, before, 0), axis=0)
    key = expert_id * capacity + rank
    slots = jnp.arange(total, dtype=I32)
    home = slots[:, None] == key[None, :]

    routed = norm_and_gate(text, norm_gain, router, expert_id)
    leaving = mm((home & ~in_image[None, :]).astype(BF16), routed).astype(BF16)
    spare = jnp.broadcast_to(expert_id.astype(BF16), (size, 8, row_count))
    slab = capacity * feature // row_count
    leaving = jnp.concatenate([leaving.reshape(size, slab, row_count), spare], axis=1)
    arrived = exchange(leaving)
    pre_blocks, arrived = lax.optimization_barrier((adapter_first(patches, fc1, size), arrived))
    all_routes = arrived[:, slab, :].astype(I32).reshape(size * row_count)
    arrived = arrived[:, :slab, :].reshape(total, feature)
    later = lax.all_gather(
        jnp.concatenate(after(leaving, fc2, proj), axis=1), "dp", axis=0, tiled=True
    )
    second_blocks = layer(exchange(pre_blocks), later, 0, fc2.shape[1], 1)

    mine = (all_routes == me).reshape(size, row_count)
    spots = jnp.arange(size * row_count, dtype=I32).reshape(size, row_count) - first
    row_image = (spots >= 0) & (spots < vis_count)
    text_count = jnp.sum((mine & ~row_image).astype(I32), axis=1)
    img_count = jnp.sum((mine & row_image).astype(I32), axis=1)
    blocks_before = jnp.arange(size)[:, None] > jnp.arange(size)[None, :]
    text_before = jnp.sum(jnp.where(blocks_before, text_count[None, :], 0), axis=1)
    img_before = jnp.sum(jnp.where(blocks_before, img_count[None, :], 0), axis=1)
    base = rows_a + jnp.maximum(jnp.sum(text_count) - rows_a, 0)
    ranks = jnp.arange(capacity, dtype=I32)[None, :]
    text_slot = ranks < text_count[:, None]
    img_slot = ~text_slot & (ranks < (text_count + img_count)[:, None])
    text_row = text_before[:, None] + ranks
    img_row = base + (img_before - text_count)[:, None] + ranks
    row_of = jnp.where(text_slot, text_row, jnp.where(img_slot, img_row, -1))
    row_of_text = jnp.where(text_slot, text_row, -1).reshape(total)
    row_of = row_of.reshape(total)
    pack = (slots[:, None] == row_of_text[None, :]).astype(BF16)
    unpack = (row_of[:, None] == slots[None, :]).astype(BF16)

    run = lambda blocks, out_rows, share=1: expert_part(blocks, out_rows, gate_w[0], up_w[0], down_w[0], share)
    chunk_a = mm(pack[:rows_a], arrived).astype(BF16)
    overflow = mm(pack[rows_a:], arrived).astype(BF16)
    half = rows_a // 2
    below, above, other = ring(chunk_a, 1), ring(chunk_a, -1), swap(chunk_a)
    own, other = after(second_blocks, chunk_a, other)
    mine, theirs = run([own, other], (rows_a, rows_a), 2)
    below, above = after(theirs, below, above)
    far_top, far_low = ring(below[:half], 1), ring(above[half:], -1)
    below_pair, above_pair = swap(below), swap(above)
    second_blocks, mine, theirs = tie(exchange(second_blocks), mine, theirs)
    third_blocks = layer(second_blocks, later, fc2.shape[1], proj.shape[1], 2)

    below, above, below_pair, above_pair, far_top, far_low = after(
        third_blocks, below, above, below_pair, above_pair, far_top, far_low
    )
    below_top, below_low, below_other, above_top, above_low, above_other = run(
        [below, below_pair, above, above_pair], (half, half, rows_a, half, half, rows_a)
    )
    far_top_pair, far_low_pair = swap(far_top), swap(far_low)
    mine_too = swap(theirs)
    visual_blocks, below_other, above_other, mine_too = tie(
        exchange(third_blocks), below_other, above_other, mine_too
    )
    visual_mine = jnp.sum(visual_blocks.astype(F32), axis=0).astype(BF16)

    visual_blocks = jnp.broadcast_to(visual_mine[None], (size, *visual_mine.shape))
    below_too, above_too = after(visual_blocks, swap(below_other), swap(above_other))
    to_above, to_below = add(above_low, above_too[half:]), add(below_top, below_too[:half])
    from_below_low, from_above_top = ring(to_above, 1), ring(to_below, -1)
    far = after(visual_blocks, far_top, far_low, far_top_pair, far_low_pair)
    far_mine_top, far_mine_low, far_theirs = run(far, (half, half, rows_a))
    visual_blocks, far_theirs, from_below_low, from_above_top, overflow = tie(
        exchange(visual_blocks), far_theirs, from_below_low, from_above_top, overflow
    )
    far_too = swap(far_theirs)
    pass_up = ring(add(far_mine_top, far_too[:half]), 1)
    pass_down = ring(add(far_mine_low, far_too[half:]), -1)
    img_routes = lax.dynamic_slice(all_routes, (first,), (vis_count,))
    named_img = (img_routes[:, None] == jnp.arange(experts_all, dtype=I32)[None, :]).astype(F32)
    mine_img = img_routes == me
    img_rank = earlier(mine_img[None, :])[0] + (base - rows_a)
    take = (jnp.arange(rows_b, dtype=I32)[:, None] == jnp.where(mine_img, img_rank, -1)[None, :]).astype(BF16)
    visual, chunk_b = visual_chunk(visual_blocks, norm_gain, router, named_img, take, overflow)
    gathered_b = lax.all_gather(chunk_b, "dp", axis=0, tiled=True)
    on_above = add(above_top, above_too[:half], pass_up)
    on_below = add(below_low, below_too[half:], pass_down)
    gathered_b, on_above, on_below = tie(gathered_b, on_above, on_below)
    from_below_top, from_above_low = ring(on_above, 1), ring(on_below, -1)
    (part_b,) = run([gathered_b], (gathered_b.shape[0],))
    done_b = lax.psum_scatter(part_b, "dp", scatter_dimension=0, tiled=True)
    top = add(mine[:half], mine_too[:half], from_below_top, from_above_top)
    low = add(mine[half:], mine_too[half:], from_below_low, from_above_low)
    done_a = jnp.concatenate([top, low])

    back = (mm(unpack[:, :rows_a], done_a) + mm(unpack[:, rows_a:], done_b)).astype(BF16)
    back = exchange(back.reshape(size, slab, row_count)).reshape(total, feature)
    turn = (((0,), (0,)), ((), ()))
    combined = lax.dot_general(home.astype(BF16), back, turn, preferred_element_type=F32)
    pick = (offsets[:, None] == jnp.arange(vis_count, dtype=I32)[None, :]).astype(BF16)
    embedded = jnp.where(in_image[:, None], mm(pick, visual), text.astype(F32))
    return (embedded + combined).astype(BF16)


def solution(mesh):
    return jax.shard_map(
        on_device,
        mesh=mesh,
        in_specs=(
            P(("dp", "expert"), None),
            P("dp", None, None, "expert"),
            P("dp"),
            P(None, "expert", "dp"),
            P("expert", "dp"),
            P("expert", "dp"),
            P(),
            P(),
            P(("dp", "expert"), None),
            P("expert", None, "dp"),
            P("expert", None, "dp"),
            P("expert", "dp", None),
        ),
        out_specs=P(("dp", "expert"), None),
        check_vma=False,
    )
```

```python
import functools

import jax
import jax.numpy as jnp
from jax import lax
from jax.experimental import pallas as pl
from jax.experimental.pallas import tpu as pltpu
from jax.sharding import PartitionSpec as P

EPSILON = 1e-05
F32 = jnp.float32
BF16 = jnp.bfloat16
I32 = jnp.int32


def mm(a, b):
    return jnp.dot(a, b, preferred_element_type=F32)


def exchange(blocks):
    return lax.all_to_all(blocks, "expert", 0, 0, tiled=True)


def cut_columns(value, size):
    rows, cols = value.shape
    return value.reshape(rows, size, cols // size).transpose(1, 0, 2)


def earlier(mask):
    n = mask.shape[-1]
    tri = (jnp.arange(n)[:, None] < jnp.arange(n)[None, :]).astype(BF16)
    return mm(mask.astype(BF16), tri).astype(I32)


def norm_and_gate(rows, norm_gain, router, expert_id):
    wide = rows.astype(F32)
    mean_square = jnp.mean(wide * wide, axis=-1, keepdims=True)
    normed = (wide * lax.rsqrt(mean_square + EPSILON) * norm_gain.astype(F32)).astype(BF16)
    logits = mm(normed, router)
    named = expert_id[:, None] == jnp.arange(router.shape[1], dtype=I32)[None, :]
    score = jax.nn.sigmoid(jnp.sum(jnp.where(named, logits, 0.0), axis=-1))
    return (normed.astype(F32) * score[:, None]).astype(BF16)


def adapter_first(patches, fc1, size):
    half = patches.shape[1] // 2
    channels = patches.shape[3]
    vis_count = half * half
    shuffled = patches.reshape(half, 2, half, 2, channels)
    shuffled = shuffled.transpose(0, 2, 1, 3, 4).reshape(vis_count, 4 * channels)
    first = lax.all_gather(fc1, "dp", axis=2, tiled=True)
    first = first.reshape(4 * channels, first.shape[2])
    return cut_columns(mm(shuffled, first).astype(BF16), size)


def layer_kernel(at, blocks_ref, weights_ref, out_ref, active, held, sems):
    parts, inner, width = held.shape

    def columns(d):
        rows = pl.ds(pl.multiple_of(d * inner, inner), inner)
        return pltpu.make_async_copy(weights_ref.at[rows, pl.ds(at, width)], held.at[d], sems.at[d])

    @pl.loop(0, parts)
    def _(d):
        columns(d).start()

    total = blocks_ref[0].astype(F32)
    for i in range(1, blocks_ref.shape[0]):
        total += blocks_ref[i].astype(F32)
    active[...] = (0.5 * total * (1.0 + lax.erf(total * (0.5**0.5)))).astype(BF16)
    size, rows, cols = out_ref.shape

    @pl.loop(0, parts)
    def _(d):
        columns(d).wait()
        part = mm(active[...], held[d]).astype(BF16)
        for i in range(size // parts):
            if cols == width:
                out_ref[i * parts + d] = part[i * rows : (i + 1) * rows]
            else:
                out_ref[d * (size // parts) + i] = part[:, i * cols : (i + 1) * cols]


def layer(blocks, weights, at, width, row_cut):
    size, tokens, inner = blocks.shape
    parts = weights.shape[0] // inner
    shape = (size, tokens // row_cut, parts * width * row_cut // size)
    return pl.pallas_call(
        functools.partial(layer_kernel, at),
        in_specs=[pl.BlockSpec(memory_space=pltpu.VMEM), pl.BlockSpec(memory_space=pl.ANY)],
        out_specs=pl.BlockSpec(memory_space=pltpu.VMEM),
        out_shape=jax.ShapeDtypeStruct(shape, BF16),
        scratch_shapes=[
            pltpu.VMEM((tokens, inner), BF16),
            pltpu.VMEM((parts, inner, width), BF16),
            pltpu.SemaphoreType.DMA((parts,)),
        ],
        compiler_params=pltpu.CompilerParams(vmem_limit_bytes=16 << 20),
        cost_estimate=pl.CostEstimate(
            flops=2 * tokens * inner * parts * width,
            bytes_accessed=2 * inner * parts * width + 4 * blocks.size,
            transcendentals=tokens * inner,
        ),
        name="layer",
    )(blocks, pltpu.with_memory_space_constraint(weights, pltpu.HBM))


def visual_kernel(blocks_ref, gain_ref, router_ref, named_ref, take_ref, base_ref, visual_ref, chunk_ref):
    size, rows, cols = blocks_ref.shape
    halves = visual_ref.shape[0] // rows
    across = size // halves
    parts = [
        jnp.concatenate([blocks_ref[r * across + c].astype(F32) for c in range(across)], axis=1)
        for r in range(halves)
    ]
    wide = jnp.concatenate(parts, axis=0)
    visual_ref[...] = wide.astype(BF16)
    mean_square = jnp.mean(wide * wide, axis=-1, keepdims=True)
    normed = (wide * lax.rsqrt(mean_square + EPSILON) * gain_ref[...].astype(F32)).astype(BF16)
    turn = (((1,), (1,)), ((), ()))
    logits = lax.dot_general(normed, router_ref[...], turn, preferred_element_type=F32)
    score = jax.nn.sigmoid(jnp.sum(named_ref[...] * logits, axis=-1, keepdims=True))
    routed = (normed.astype(F32) * score).astype(BF16)
    chunk_ref[...] = (base_ref[...].astype(F32) + mm(take_ref[...], routed)).astype(BF16)


def visual_chunk(blocks, norm_gain, router, named, take, base):
    size, rows, cols = blocks.shape
    feature = router.shape[0]
    tokens = size * rows * cols // feature
    return pl.pallas_call(
        visual_kernel,
        in_specs=[pl.BlockSpec(memory_space=pltpu.VMEM)] * 6,
        out_specs=[pl.BlockSpec(memory_space=pltpu.VMEM)] * 2,
        out_shape=[
            jax.ShapeDtypeStruct((tokens, feature), BF16),
            jax.ShapeDtypeStruct((take.shape[0], feature), BF16),
        ],
        compiler_params=pltpu.CompilerParams(vmem_limit_bytes=24 << 20),
        cost_estimate=pl.CostEstimate(
            flops=2 * tokens * feature * 64, bytes_accessed=8 * tokens * feature, transcendentals=tokens
        ),
        name="visual_chunk",
    )(blocks, norm_gain[None, :], router.T, named, take, base)


CHUNK = 1280
ROW_TILE = 256


def span(index, length):
    return pl.ds(pl.multiple_of(index * length, length), length)


def expert_kernel(in_count, *refs):
    blocks = refs[:in_count]
    weights = refs[in_count : in_count + 3]
    outs = refs[in_count + 3 : -10]
    rows, gate_v, up_v, down_v, gate_acc, up_acc, hidden, in_sem, w_sem, out_sem = refs[-10:]
    feature = rows.shape[1]
    chunks = feature // CHUNK
    tiles = rows.shape[0] // ROW_TILE

    def blocks_in():
        at = 0
        for i, block in enumerate(blocks):
            yield pltpu.make_async_copy(block, rows.at[pl.ds(at, block.shape[0])], in_sem.at[i])
            at += block.shape[0]

    def inner(which, k):
        held = (gate_v, up_v)[which]
        return pltpu.make_async_copy(weights[which].at[span(k, CHUNK)], held.at[span(k, CHUNK)], w_sem.at[which, k])

    def outer(k):
        return pltpu.make_async_copy(weights[2].at[:, span(k, CHUNK)], down_v.at[:, span(k, CHUNK)], w_sem.at[2, k])

    def leaving(k):
        at = 0
        for i, out in enumerate(outs):
            count = out.shape[0]
            yield pltpu.make_async_copy(
                rows.at[pl.ds(at, count), span(k, CHUNK)], out.at[:, span(k, CHUNK)], out_sem.at[i, k]
            )
            at += count

    for copy in blocks_in():
        copy.start()

    @pl.loop(0, chunks)
    def _(k):
        inner(0, k).start()
        inner(1, k).start()

    @pl.loop(0, chunks)
    def _(k):
        outer(k).start()

    for copy in blocks_in():
        copy.wait()
    gate_acc[...] = jnp.zeros_like(gate_acc)
    up_acc[...] = jnp.zeros_like(up_acc)

    @pl.loop(0, chunks)
    def _(k):
        inner(0, k).wait()
        inner(1, k).wait()

        @pl.loop(0, tiles)
        def _(t):
            part = rows[span(t, ROW_TILE), span(k, CHUNK)]
            gate_acc[span(t, ROW_TILE), :] += mm(part, gate_v[span(k, CHUNK), :])
            up_acc[span(t, ROW_TILE), :] += mm(part, up_v[span(k, CHUNK), :])

    hidden[...] = (jax.nn.silu(gate_acc[...]) * up_acc[...]).astype(BF16)

    @pl.loop(0, chunks)
    def _(k):
        outer(k).wait()

        @pl.loop(0, tiles)
        def _(t):
            made = mm(hidden[span(t, ROW_TILE), :], down_v[:, span(k, CHUNK)])
            rows[span(t, ROW_TILE), span(k, CHUNK)] = made.astype(BF16)

        for copy in leaving(k):
            copy.start()

    @pl.loop(0, chunks)
    def _(k):
        for copy in leaving(k):
            copy.wait()


def expert_part(blocks, out_rows, gate_w, up_w, down_w, share=1):
    feature, width = gate_w.shape
    count = sum(block.shape[0] for block in blocks)
    chunks = feature // CHUNK
    weights = [pltpu.with_memory_space_constraint(w, pltpu.HBM) for w in (gate_w, up_w, down_w)]
    anywhere = pl.BlockSpec(memory_space=pl.ANY)
    return pl.pallas_call(
        functools.partial(expert_kernel, len(blocks)),
        in_specs=[anywhere] * (len(blocks) + 3),
        out_specs=[pl.BlockSpec(memory_space=pltpu.HBM)] * len(out_rows),
        out_shape=[pltpu.HBM((rows, feature), BF16) for rows in out_rows],
        scratch_shapes=[
            pltpu.VMEM((count, feature), BF16),
            pltpu.VMEM((feature, width), BF16),
            pltpu.VMEM((feature, width), BF16),
            pltpu.VMEM((width, feature), BF16),
            pltpu.VMEM((count, width), F32),
            pltpu.VMEM((count, width), F32),
            pltpu.VMEM((count, width), BF16),
            pltpu.SemaphoreType.DMA((len(blocks),)),
            pltpu.SemaphoreType.DMA((3, chunks)),
            pltpu.SemaphoreType.DMA((len(out_rows), chunks)),
        ],
        compiler_params=pltpu.CompilerParams(vmem_limit_bytes=28 << 20),
        cost_estimate=pl.CostEstimate(
            flops=6 * count * feature * width // share,
            bytes_accessed=(6 * feature * width + 4 * count * feature) // share,
            transcendentals=count * width // share,
        ),
        name="expert_part",
    )(*[pltpu.with_memory_space_constraint(block, pltpu.HBM) for block in blocks], *weights)


def ring(value, step):
    size = lax.axis_size("dp")
    return lax.ppermute(value, "dp", [(i, (i + 2 * step) % size) for i in range(size)])


def swap(value):
    size = lax.axis_size("dp")
    return lax.ppermute(value, "dp", [(i, i ^ 1) for i in range(size)])


def tie(*values):
    return lax.optimization_barrier(values)


def after(first, *values):
    return lax.optimization_barrier((*values, first))[:-1]


def add(*terms):
    total = terms[0].astype(F32)
    for term in terms[1:]:
        total = total + term.astype(F32)
    return total.astype(BF16)


def on_device(
    text, patches, vis_start, fc1, fc2, proj, norm_gain, router, routes, gate_w, up_w, down_w
):
    size = lax.axis_size("expert")
    me = lax.axis_index("expert")
    row_count, feature = text.shape
    experts_all = router.shape[1]
    vis_count = (patches.shape[1] // 2) ** 2
    capacity = max(2, row_count * 5 // (4 * size))
    first = vis_start[0]
    expert_id = routes[:, 0]
    total = size * capacity
    rows_a = size * (capacity // 8 * 8)
    rows_b = total - rows_a

    lanes = jnp.arange(row_count, dtype=I32)
    offsets = me * row_count + lanes - first
    in_image = (offsets >= 0) & (offsets < vis_count)
    named = jnp.arange(experts_all, dtype=I32)[:, None] == expert_id[None, :]
    named_text = named & ~in_image[None, :]
    named_img = named & in_image[None, :]
    text_total = jnp.sum(named_text.astype(I32), axis=1, keepdims=True)
    before = jnp.where(in_image[None, :], earlier(named_img) + text_total, earlier(named_text))
    rank = jnp.sum(jnp.where(named, before, 0), axis=0)
    key = expert_id * capacity + rank
    slots = jnp.arange(total, dtype=I32)
    home = slots[:, None] == key[None, :]

    routed = norm_and_gate(text, norm_gain, router, expert_id)
    leaving = mm((home & ~in_image[None, :]).astype(BF16), routed).astype(BF16)
    spare = jnp.broadcast_to(expert_id.astype(BF16), (size, 8, row_count))
    slab = capacity * feature // row_count
    leaving = jnp.concatenate([leaving.reshape(size, slab, row_count), spare], axis=1)
    arrived = exchange(leaving)
    pre_blocks, arrived = lax.optimization_barrier((adapter_first(patches, fc1, size), arrived))
    all_routes = arrived[:, slab, :].astype(I32).reshape(size * row_count)
    arrived = arrived[:, :slab, :].reshape(total, feature)
    later = lax.all_gather(
        jnp.concatenate(after(leaving, fc2, proj), axis=1), "dp", axis=0, tiled=True
    )
    second_blocks = layer(exchange(pre_blocks), later, 0, fc2.shape[1], 1)

    mine = (all_routes == me).reshape(size, row_count)
    spots = jnp.arange(size * row_count, dtype=I32).reshape(size, row_count) - first
    row_image = (spots >= 0) & (spots < vis_count)
    text_count = jnp.sum((mine & ~row_image).astype(I32), axis=1)
    img_count = jnp.sum((mine & row_image).astype(I32), axis=1)
    blocks_before = jnp.arange(size)[:, None] > jnp.arange(size)[None, :]
    text_before = jnp.sum(jnp.where(blocks_before, text_count[None, :], 0), axis=1)
    img_before = jnp.sum(jnp.where(blocks_before, img_count[None, :], 0), axis=1)
    base = rows_a + jnp.maximum(jnp.sum(text_count) - rows_a, 0)
    ranks = jnp.arange(capacity, dtype=I32)[None, :]
    text_slot = ranks < text_count[:, None]
    img_slot = ~text_slot & (ranks < (text_count + img_count)[:, None])
    text_row = text_before[:, None] + ranks
    img_row = base + (img_before - text_count)[:, None] + ranks
    row_of = jnp.where(text_slot, text_row, jnp.where(img_slot, img_row, -1))
    row_of_text = jnp.where(text_slot, text_row, -1).reshape(total)
    row_of = row_of.reshape(total)
    pack = (slots[:, None] == row_of_text[None, :]).astype(BF16)
    unpack = (row_of[:, None] == slots[None, :]).astype(BF16)

    run = lambda blocks, out_rows, share=1: expert_part(blocks, out_rows, gate_w[0], up_w[0], down_w[0], share)
    chunk_a = mm(pack[:rows_a], arrived).astype(BF16)
    overflow = mm(pack[rows_a:], arrived).astype(BF16)
    half = rows_a // 2
    below, above, other = ring(chunk_a, 1), ring(chunk_a, -1), swap(chunk_a)
    own, other = after(second_blocks, chunk_a, other)
    mine, theirs = run([own, other], (rows_a, rows_a), 2)
    below, above = after(theirs, below, above)
    far_top, far_low = ring(below[:half], 1), ring(above[half:], -1)
    below_pair, above_pair = swap(below), swap(above)
    second_blocks, mine, theirs = tie(exchange(second_blocks), mine, theirs)
    third_blocks = layer(second_blocks, later, fc2.shape[1], proj.shape[1], 2)

    below, above, below_pair, above_pair, far_top, far_low = after(
        third_blocks, below, above, below_pair, above_pair, far_top, far_low
    )
    below_top, below_low, below_other, above_top, above_low, above_other = run(
        [below, below_pair, above, above_pair], (half, half, rows_a, half, half, rows_a)
    )
    far_top_pair, far_low_pair = swap(far_top), swap(far_low)
    mine_too = swap(theirs)
    visual_blocks, below_other, above_other, mine_too = tie(
        exchange(third_blocks), below_other, above_other, mine_too
    )
    visual_mine = jnp.sum(visual_blocks.astype(F32), axis=0).astype(BF16)

    visual_blocks = jnp.broadcast_to(visual_mine[None], (size, *visual_mine.shape))
    below_too, above_too = after(visual_blocks, swap(below_other), swap(above_other))
    to_above, to_below = add(above_low, above_too[half:]), add(below_top, below_too[:half])
    from_below_low, from_above_top = ring(to_above, 1), ring(to_below, -1)
    far = after(visual_blocks, far_top, far_low, far_top_pair, far_low_pair)
    far_mine_top, far_mine_low, far_theirs = run(far, (half, half, rows_a))
    visual_blocks, far_theirs, from_below_low, from_above_top, overflow = tie(
        exchange(visual_blocks), far_theirs, from_below_low, from_above_top, overflow
    )
    far_too = swap(far_theirs)
    pass_up = ring(add(far_mine_top, far_too[:half]), 1)
    pass_down = ring(add(far_mine_low, far_too[half:]), -1)
    img_routes = lax.dynamic_slice(all_routes, (first,), (vis_count,))
    named_img = (img_routes[:, None] == jnp.arange(experts_all, dtype=I32)[None, :]).astype(F32)
    mine_img = img_routes == me
    img_rank = earlier(mine_img[None, :])[0] + (base - rows_a)
    take = (jnp.arange(rows_b, dtype=I32)[:, None] == jnp.where(mine_img, img_rank, -1)[None, :]).astype(BF16)
    visual, chunk_b = visual_chunk(visual_blocks, norm_gain, router, named_img, take, overflow)
    gathered_b = lax.all_gather(chunk_b, "dp", axis=0, tiled=True)
    on_above = add(above_top, above_too[:half], pass_up)
    on_below = add(below_low, below_too[half:], pass_down)
    gathered_b, on_above, on_below = tie(gathered_b, on_above, on_below)
    from_below_top, from_above_low = ring(on_above, 1), ring(on_below, -1)
    (part_b,) = run([gathered_b], (gathered_b.shape[0],))
    done_b = lax.psum_scatter(part_b, "dp", scatter_dimension=0, tiled=True)
    top = add(mine[:half], mine_too[:half], from_below_top, from_above_top)
    low = add(mine[half:], mine_too[half:], from_below_low, from_above_low)
    done_a = jnp.concatenate([top, low])

    (back_a,) = tie(mm(unpack[:, :rows_a], done_a))
    back = (back_a + mm(unpack[:, rows_a:], done_b)).astype(BF16)
    back = exchange(back.reshape(size, slab, row_count)).reshape(total, feature)
    turn = (((0,), (0,)), ((), ()))
    combined = lax.dot_general(home.astype(BF16), back, turn, preferred_element_type=F32)
    pick = (offsets[:, None] == jnp.arange(vis_count, dtype=I32)[None, :]).astype(BF16)
    embedded = jnp.where(in_image[:, None], mm(pick, visual), text.astype(F32))
    return (embedded + combined).astype(BF16)


def solution(mesh):
    return jax.shard_map(
        on_device,
        mesh=mesh,
        in_specs=(
            P(("dp", "expert"), None),
            P("dp", None, None, "expert"),
            P("dp"),
            P(None, "expert", "dp"),
            P("expert", "dp"),
            P("expert", "dp"),
            P(),
            P(),
            P(("dp", "expert"), None),
            P("expert", None, "dp"),
            P("expert", None, "dp"),
            P("expert", "dp", None),
        ),
        out_specs=P(("dp", "expert"), None),
        check_vma=False,
    )
```

```python
import functools

import jax
import jax.numpy as jnp
from jax import lax
from jax.experimental import pallas as pl
from jax.experimental.pallas import tpu as pltpu
from jax.sharding import PartitionSpec as P

EPSILON = 1e-05
F32 = jnp.float32
BF16 = jnp.bfloat16
I32 = jnp.int32


def mm(a, b):
    return jnp.dot(a, b, preferred_element_type=F32)


def exchange(blocks):
    return lax.all_to_all(blocks, "expert", 0, 0, tiled=True)


def cut_columns(value, size):
    rows, cols = value.shape
    return value.reshape(rows, size, cols // size).transpose(1, 0, 2)


def earlier(mask):
    n = mask.shape[-1]
    tri = (jnp.arange(n)[:, None] < jnp.arange(n)[None, :]).astype(BF16)
    return mm(mask.astype(BF16), tri).astype(I32)


def norm_and_gate(rows, norm_gain, router, expert_id):
    wide = rows.astype(F32)
    mean_square = jnp.mean(wide * wide, axis=-1, keepdims=True)
    normed = (wide * lax.rsqrt(mean_square + EPSILON) * norm_gain.astype(F32)).astype(BF16)
    logits = mm(normed, router)
    named = expert_id[:, None] == jnp.arange(router.shape[1], dtype=I32)[None, :]
    score = jax.nn.sigmoid(jnp.sum(jnp.where(named, logits, 0.0), axis=-1))
    return (normed.astype(F32) * score[:, None]).astype(BF16)


def adapter_first(patches, fc1, size):
    half = patches.shape[1] // 2
    channels = patches.shape[3]
    vis_count = half * half
    shuffled = patches.reshape(half, 2, half, 2, channels)
    shuffled = shuffled.transpose(0, 2, 1, 3, 4).reshape(vis_count, 4 * channels)
    first = lax.all_gather(fc1, "dp", axis=2, tiled=True)
    first = first.reshape(4 * channels, first.shape[2])
    return cut_columns(mm(shuffled, first).astype(BF16), size)


def layer_kernel(at, blocks_ref, weights_ref, out_ref, active, held, sems):
    parts, inner, width = held.shape

    def columns(d):
        rows = pl.ds(pl.multiple_of(d * inner, inner), inner)
        return pltpu.make_async_copy(weights_ref.at[rows, pl.ds(at, width)], held.at[d], sems.at[d])

    @pl.loop(0, parts)
    def _(d):
        columns(d).start()

    total = blocks_ref[0].astype(F32)
    for i in range(1, blocks_ref.shape[0]):
        total += blocks_ref[i].astype(F32)
    active[...] = (0.5 * total * (1.0 + lax.erf(total * (0.5**0.5)))).astype(BF16)
    size, rows, cols = out_ref.shape

    @pl.loop(0, parts)
    def _(d):
        columns(d).wait()
        part = mm(active[...], held[d]).astype(BF16)
        for i in range(size // parts):
            if cols == width:
                out_ref[i * parts + d] = part[i * rows : (i + 1) * rows]
            else:
                out_ref[d * (size // parts) + i] = part[:, i * cols : (i + 1) * cols]


def layer(blocks, weights, at, width, row_cut):
    size, tokens, inner = blocks.shape
    parts = weights.shape[0] // inner
    shape = (size, tokens // row_cut, parts * width * row_cut // size)
    return pl.pallas_call(
        functools.partial(layer_kernel, at),
        in_specs=[pl.BlockSpec(memory_space=pltpu.VMEM), pl.BlockSpec(memory_space=pl.ANY)],
        out_specs=pl.BlockSpec(memory_space=pltpu.VMEM),
        out_shape=jax.ShapeDtypeStruct(shape, BF16),
        scratch_shapes=[
            pltpu.VMEM((tokens, inner), BF16),
            pltpu.VMEM((parts, inner, width), BF16),
            pltpu.SemaphoreType.DMA((parts,)),
        ],
        compiler_params=pltpu.CompilerParams(vmem_limit_bytes=16 << 20),
        cost_estimate=pl.CostEstimate(
            flops=2 * tokens * inner * parts * width,
            bytes_accessed=2 * inner * parts * width + 4 * blocks.size,
            transcendentals=tokens * inner,
        ),
        name="layer",
    )(blocks, pltpu.with_memory_space_constraint(weights, pltpu.HBM))


def visual_kernel(blocks_ref, gain_ref, router_ref, named_ref, take_ref, base_ref, visual_ref, chunk_ref):
    size, rows, cols = blocks_ref.shape
    halves = visual_ref.shape[0] // rows
    across = size // halves
    parts = [
        jnp.concatenate([blocks_ref[r * across + c].astype(F32) for c in range(across)], axis=1)
        for r in range(halves)
    ]
    wide = jnp.concatenate(parts, axis=0)
    visual_ref[...] = wide.astype(BF16)
    mean_square = jnp.mean(wide * wide, axis=-1, keepdims=True)
    normed = (wide * lax.rsqrt(mean_square + EPSILON) * gain_ref[...].astype(F32)).astype(BF16)
    turn = (((1,), (1,)), ((), ()))
    logits = lax.dot_general(normed, router_ref[...], turn, preferred_element_type=F32)
    score = jax.nn.sigmoid(jnp.sum(named_ref[...] * logits, axis=-1, keepdims=True))
    routed = (normed.astype(F32) * score).astype(BF16)
    chunk_ref[...] = (base_ref[...].astype(F32) + mm(take_ref[...], routed)).astype(BF16)


def visual_chunk(blocks, norm_gain, router, named, take, base):
    size, rows, cols = blocks.shape
    feature = router.shape[0]
    tokens = size * rows * cols // feature
    return pl.pallas_call(
        visual_kernel,
        in_specs=[pl.BlockSpec(memory_space=pltpu.VMEM)] * 6,
        out_specs=[pl.BlockSpec(memory_space=pltpu.VMEM)] * 2,
        out_shape=[
            jax.ShapeDtypeStruct((tokens, feature), BF16),
            jax.ShapeDtypeStruct((take.shape[0], feature), BF16),
        ],
        compiler_params=pltpu.CompilerParams(vmem_limit_bytes=24 << 20),
        cost_estimate=pl.CostEstimate(
            flops=2 * tokens * feature * 64, bytes_accessed=8 * tokens * feature, transcendentals=tokens
        ),
        name="visual_chunk",
    )(blocks, norm_gain[None, :], router.T, named, take, base)


CHUNK = 1280
ROW_TILE = 256


def span(index, length):
    return pl.ds(pl.multiple_of(index * length, length), length)


def expert_kernel(in_count, *refs):
    blocks = refs[:in_count]
    weights = refs[in_count : in_count + 3]
    outs = refs[in_count + 3 : -10]
    rows, gate_v, up_v, down_v, gate_acc, up_acc, hidden, in_sem, w_sem, out_sem = refs[-10:]
    feature = rows.shape[1]
    chunks = feature // CHUNK
    tiles = rows.shape[0] // ROW_TILE

    def blocks_in():
        at = 0
        for i, block in enumerate(blocks):
            yield pltpu.make_async_copy(block, rows.at[pl.ds(at, block.shape[0])], in_sem.at[i])
            at += block.shape[0]

    def inner(which, k):
        held = (gate_v, up_v)[which]
        return pltpu.make_async_copy(weights[which].at[span(k, CHUNK)], held.at[span(k, CHUNK)], w_sem.at[which, k])

    def outer(k):
        return pltpu.make_async_copy(weights[2].at[:, span(k, CHUNK)], down_v.at[:, span(k, CHUNK)], w_sem.at[2, k])

    def leaving(k):
        at = 0
        for i, out in enumerate(outs):
            count = out.shape[0]
            yield pltpu.make_async_copy(
                rows.at[pl.ds(at, count), span(k, CHUNK)], out.at[:, span(k, CHUNK)], out_sem.at[i, k]
            )
            at += count

    for copy in blocks_in():
        copy.start()

    @pl.loop(0, chunks)
    def _(k):
        inner(0, k).start()
        inner(1, k).start()

    @pl.loop(0, chunks)
    def _(k):
        outer(k).start()

    for copy in blocks_in():
        copy.wait()
    gate_acc[...] = jnp.zeros_like(gate_acc)
    up_acc[...] = jnp.zeros_like(up_acc)

    @pl.loop(0, chunks)
    def _(k):
        inner(0, k).wait()
        inner(1, k).wait()

        @pl.loop(0, tiles)
        def _(t):
            part = rows[span(t, ROW_TILE), span(k, CHUNK)]
            gate_acc[span(t, ROW_TILE), :] += mm(part, gate_v[span(k, CHUNK), :])
            up_acc[span(t, ROW_TILE), :] += mm(part, up_v[span(k, CHUNK), :])

    hidden[...] = (jax.nn.silu(gate_acc[...]) * up_acc[...]).astype(BF16)

    @pl.loop(0, chunks)
    def _(k):
        outer(k).wait()

        @pl.loop(0, tiles)
        def _(t):
            made = mm(hidden[span(t, ROW_TILE), :], down_v[:, span(k, CHUNK)])
            rows[span(t, ROW_TILE), span(k, CHUNK)] = made.astype(BF16)

        for copy in leaving(k):
            copy.start()

    @pl.loop(0, chunks)
    def _(k):
        for copy in leaving(k):
            copy.wait()


def expert_part(blocks, out_rows, gate_w, up_w, down_w, share=1):
    feature, width = gate_w.shape
    count = sum(block.shape[0] for block in blocks)
    chunks = feature // CHUNK
    weights = [pltpu.with_memory_space_constraint(w, pltpu.HBM) for w in (gate_w, up_w, down_w)]
    anywhere = pl.BlockSpec(memory_space=pl.ANY)
    return pl.pallas_call(
        functools.partial(expert_kernel, len(blocks)),
        in_specs=[anywhere] * (len(blocks) + 3),
        out_specs=[pl.BlockSpec(memory_space=pltpu.HBM)] * len(out_rows),
        out_shape=[pltpu.HBM((rows, feature), BF16) for rows in out_rows],
        scratch_shapes=[
            pltpu.VMEM((count, feature), BF16),
            pltpu.VMEM((feature, width), BF16),
            pltpu.VMEM((feature, width), BF16),
            pltpu.VMEM((width, feature), BF16),
            pltpu.VMEM((count, width), F32),
            pltpu.VMEM((count, width), F32),
            pltpu.VMEM((count, width), BF16),
            pltpu.SemaphoreType.DMA((len(blocks),)),
            pltpu.SemaphoreType.DMA((3, chunks)),
            pltpu.SemaphoreType.DMA((len(out_rows), chunks)),
        ],
        compiler_params=pltpu.CompilerParams(vmem_limit_bytes=28 << 20),
        cost_estimate=pl.CostEstimate(
            flops=6 * count * feature * width // share,
            bytes_accessed=(6 * feature * width + 4 * count * feature) // share,
            transcendentals=count * width // share,
        ),
        name="expert_part",
    )(*[pltpu.with_memory_space_constraint(block, pltpu.HBM) for block in blocks], *weights)


def ring(value, step):
    size = lax.axis_size("dp")
    return lax.ppermute(value, "dp", [(i, (i + 2 * step) % size) for i in range(size)])


def swap(value):
    size = lax.axis_size("dp")
    return lax.ppermute(value, "dp", [(i, i ^ 1) for i in range(size)])


def tie(*values):
    return lax.optimization_barrier(values)


def after(first, *values):
    return lax.optimization_barrier((*values, first))[:-1]


def add(*terms):
    total = terms[0].astype(F32)
    for term in terms[1:]:
        total = total + term.astype(F32)
    return total.astype(BF16)


def on_device(
    text, patches, vis_start, fc1, fc2, proj, norm_gain, router, routes, gate_w, up_w, down_w
):
    size = lax.axis_size("expert")
    me = lax.axis_index("expert")
    row_count, feature = text.shape
    experts_all = router.shape[1]
    vis_count = (patches.shape[1] // 2) ** 2
    capacity = max(2, row_count * 5 // (4 * size))
    first = vis_start[0]
    expert_id = routes[:, 0]
    total = size * capacity
    rows_a = size * (capacity // 8 * 8)
    rows_b = total - rows_a

    lanes = jnp.arange(row_count, dtype=I32)
    offsets = me * row_count + lanes - first
    in_image = (offsets >= 0) & (offsets < vis_count)
    named = jnp.arange(experts_all, dtype=I32)[:, None] == expert_id[None, :]
    named_text = named & ~in_image[None, :]
    named_img = named & in_image[None, :]
    text_total = jnp.sum(named_text.astype(I32), axis=1, keepdims=True)
    before = jnp.where(in_image[None, :], earlier(named_img) + text_total, earlier(named_text))
    rank = jnp.sum(jnp.where(named, before, 0), axis=0)
    key = expert_id * capacity + rank
    slots = jnp.arange(total, dtype=I32)
    home = slots[:, None] == key[None, :]

    routed = norm_and_gate(text, norm_gain, router, expert_id)
    leaving = mm((home & ~in_image[None, :]).astype(BF16), routed).astype(BF16)
    spare = jnp.broadcast_to(expert_id.astype(BF16), (size, 8, row_count))
    slab = capacity * feature // row_count
    leaving = jnp.concatenate([leaving.reshape(size, slab, row_count), spare], axis=1)
    arrived = exchange(leaving)
    pre_blocks, arrived = lax.optimization_barrier((adapter_first(patches, fc1, size), arrived))
    all_routes = arrived[:, slab, :].astype(I32).reshape(size * row_count)
    arrived = arrived[:, :slab, :].reshape(total, feature)
    later = lax.all_gather(
        jnp.concatenate(after(leaving, fc2, proj), axis=1), "dp", axis=0, tiled=True
    )
    second_blocks = layer(exchange(pre_blocks), later, 0, fc2.shape[1], 1)

    mine = (all_routes == me).reshape(size, row_count)
    spots = jnp.arange(size * row_count, dtype=I32).reshape(size, row_count) - first
    row_image = (spots >= 0) & (spots < vis_count)
    text_count = jnp.sum((mine & ~row_image).astype(I32), axis=1)
    img_count = jnp.sum((mine & row_image).astype(I32), axis=1)
    blocks_before = jnp.arange(size)[:, None] > jnp.arange(size)[None, :]
    text_before = jnp.sum(jnp.where(blocks_before, text_count[None, :], 0), axis=1)
    img_before = jnp.sum(jnp.where(blocks_before, img_count[None, :], 0), axis=1)
    base = rows_a + jnp.maximum(jnp.sum(text_count) - rows_a, 0)
    ranks = jnp.arange(capacity, dtype=I32)[None, :]
    text_slot = ranks < text_count[:, None]
    img_slot = ~text_slot & (ranks < (text_count + img_count)[:, None])
    text_row = text_before[:, None] + ranks
    img_row = base + (img_before - text_count)[:, None] + ranks
    row_of = jnp.where(text_slot, text_row, jnp.where(img_slot, img_row, -1))
    row_of_text = jnp.where(text_slot, text_row, -1).reshape(total)
    row_of = row_of.reshape(total)
    pack = (slots[:, None] == row_of_text[None, :]).astype(BF16)
    unpack = (row_of[:, None] == slots[None, :]).astype(BF16)

    run = lambda blocks, out_rows, share=1: expert_part(blocks, out_rows, gate_w[0], up_w[0], down_w[0], share)
    chunk_a = mm(pack[:rows_a], arrived).astype(BF16)
    overflow = mm(pack[rows_a:], arrived).astype(BF16)
    half = rows_a // 2
    below, above, other = ring(chunk_a, 1), ring(chunk_a, -1), swap(chunk_a)
    own, other = after(second_blocks, chunk_a, other)
    mine, theirs = run([own, other], (rows_a, rows_a), 2)
    below, above = after(theirs, below, above)
    far_top, far_low = ring(below[:half], 1), ring(above[half:], -1)
    below_pair, above_pair = swap(below), swap(above)
    second_blocks, mine, theirs = tie(exchange(second_blocks), mine, theirs)
    third_blocks = layer(second_blocks, later, fc2.shape[1], proj.shape[1], 2)

    below, above, below_pair, above_pair, far_top, far_low = after(
        third_blocks, below, above, below_pair, above_pair, far_top, far_low
    )
    below_top, below_low, below_other, above_top, above_low, above_other = run(
        [below, below_pair, above, above_pair], (half, half, rows_a, half, half, rows_a)
    )
    far_top_pair, far_low_pair = swap(far_top), swap(far_low)
    mine_too = swap(theirs)
    visual_blocks, below_other, above_other, mine_too = tie(
        exchange(third_blocks), below_other, above_other, mine_too
    )
    visual_mine = jnp.sum(visual_blocks.astype(F32), axis=0).astype(BF16)

    visual_blocks = jnp.broadcast_to(visual_mine[None], (size, *visual_mine.shape))
    below_too, above_too = after(visual_blocks, swap(below_other), swap(above_other))
    to_above, to_below = add(above_low, above_too[half:]), add(below_top, below_too[:half])
    from_below_low, from_above_top = ring(to_above, 1), ring(to_below, -1)
    far = after(visual_blocks, far_top, far_low, far_top_pair, far_low_pair)
    far_mine_top, far_mine_low, far_theirs = run(far, (half, half, rows_a))
    visual_blocks, far_theirs, from_below_low, from_above_top, overflow = tie(
        exchange(visual_blocks), far_theirs, from_below_low, from_above_top, overflow
    )
    far_too = swap(far_theirs)
    pass_up = ring(add(far_mine_top, far_too[:half]), 1)
    pass_down = ring(add(far_mine_low, far_too[half:]), -1)
    img_routes = lax.dynamic_slice(all_routes, (first,), (vis_count,))
    named_img = (img_routes[:, None] == jnp.arange(experts_all, dtype=I32)[None, :]).astype(F32)
    mine_img = img_routes == me
    img_rank = earlier(mine_img[None, :])[0] + (base - rows_a)
    take = (jnp.arange(rows_b, dtype=I32)[:, None] == jnp.where(mine_img, img_rank, -1)[None, :]).astype(BF16)
    visual, chunk_b = visual_chunk(visual_blocks, norm_gain, router, named_img, take, overflow)
    gathered_b = lax.all_gather(chunk_b, "dp", axis=0, tiled=True)
    gathered_b, pass_up, pass_down = tie(gathered_b, pass_up, pass_down)
    on_above = add(above_top, above_too[:half], pass_up)
    on_below = add(below_low, below_too[half:], pass_down)
    from_below_top, from_above_low = ring(on_above, 1), ring(on_below, -1)
    (part_b,) = run([gathered_b], (gathered_b.shape[0],))
    done_b = lax.psum_scatter(part_b, "dp", scatter_dimension=0, tiled=True)
    top = add(mine[:half], mine_too[:half], from_below_top, from_above_top)
    low = add(mine[half:], mine_too[half:], from_below_low, from_above_low)
    done_a = jnp.concatenate([top, low])

    back = (mm(unpack[:, :rows_a], done_a) + mm(unpack[:, rows_a:], done_b)).astype(BF16)
    back = exchange(back.reshape(size, slab, row_count)).reshape(total, feature)
    turn = (((0,), (0,)), ((), ()))
    combined = lax.dot_general(home.astype(BF16), back, turn, preferred_element_type=F32)
    pick = (offsets[:, None] == jnp.arange(vis_count, dtype=I32)[None, :]).astype(BF16)
    embedded = jnp.where(in_image[:, None], mm(pick, visual), text.astype(F32))
    return (embedded + combined).astype(BF16)


def solution(mesh):
    return jax.shard_map(
        on_device,
        mesh=mesh,
        in_specs=(
            P(("dp", "expert"), None),
            P("dp", None, None, "expert"),
            P("dp"),
            P(None, "expert", "dp"),
            P("expert", "dp"),
            P("expert", "dp"),
            P(),
            P(),
            P(("dp", "expert"), None),
            P("expert", None, "dp"),
            P("expert", None, "dp"),
            P("expert", "dp", None),
        ),
        out_specs=P(("dp", "expert"), None),
        check_vma=False,
    )
```
